512 devices in a mesh: clu: 64 (over x, z), grp: 8 (over y, core).
Axes of the slice: x: 4, y: 4, z: 16, core: 2. Of those that a mesh axis runs over, the one named last changes fastest.
Arguments:
- embeddings: bfloat16 [65536, 512], P(('clu', 'grp')), may hold values from -60 to 60
- cluster_id: int32 [65536], P(('clu', 'grp')), may hold values from 0 to 255, as said below
- cluster_group: int32 [256], replicated, may hold values from 0 to 63, as said below
Outputs:
- best_similarity: float32 [65536], P(('clu', 'grp'))
The draws below stay inside these ranges and needn't reach their ends.
Inputs may be any that keep to these rules, and one draw needn't show every extreme that they name: `cluster_id`: on every device's rows, at most 8 rows belong to clusters of one group, and exactly 8 for some group. `cluster_group`: every group is named by exactly 4 clusters.
All inputs are finite; a program needn't handle non-finite values.
Results may differ from the reference program's by a relative error of at most 0.0015.
Values may be sent and summed in bfloat16 or wider, within the bound.
A program may use at most 64 MiB of HBM per device.

```python
import jax
import jax.numpy as jnp
from jax import lax

D = 512
ROWS_DEV = 128
K_G = 4
GROUP_ROW_LIMIT = 8
CLUSTERS = 256
ROWS = 65536
N_CLU = 64
N_GRP = 8


def routing(key):
    group_table = CLUSTERS // K_G
    device_list = ROWS // ROWS_DEV
    slot_total = group_table * GROUP_ROW_LIMIT
    perm = jax.random.permutation(jax.random.fold_in(key, 11), CLUSTERS).astype(jnp.int32)
    group_of = perm // K_G
    inverse = jnp.zeros((CLUSTERS,), jnp.int32).at[perm].set(jnp.arange(CLUSTERS, dtype=jnp.int32))
    load_pressure = jax.random.randint(jax.random.fold_in(key, 12), (group_table,), 0, 2 ** 14)
    random_jitter = jax.random.randint(jax.random.fold_in(key, 13), (device_list, slot_total), 0, 2 ** 14)
    pinned_choice = jax.random.randint(jax.random.fold_in(key, 14), (device_list,), 0, group_table)
    slot_owner_group = jnp.arange(slot_total, dtype=jnp.int32) // GROUP_ROW_LIMIT
    reward_term = jnp.where(slot_owner_group[None, :] == pinned_choice[:, None], 2 ** 17, 0)
    fitness_value = (random_jitter + load_pressure[slot_owner_group][None, :] + reward_term) * slot_total + jnp.arange(slot_total, dtype=jnp.int32)[None, :]
    _, chosen = lax.top_k(fitness_value, ROWS_DEV)
    shuffle = jax.random.permutation(jax.random.fold_in(key, 15), ROWS_DEV).astype(jnp.int32)
    chosen = chosen[:, shuffle]
    dest = chosen // GROUP_ROW_LIMIT
    first = jax.random.randint(jax.random.fold_in(key, 16), (device_list, ROWS_DEV), 0, K_G)
    second = jax.random.randint(jax.random.fold_in(key, 17), (device_list, ROWS_DEV), 0, K_G)
    sub = jnp.minimum(first, second)
    cluster = inverse[dest * K_G + sub]
    return (group_of.astype(jnp.int32), cluster.reshape(ROWS).astype(jnp.int32))


def draw_cluster_id(key, part):
    return routing(key)[1]


def draw_cluster_group(key, part):
    return routing(key)[0]


def draw_embeddings(key, part):
    entries = jnp.clip(jax.random.normal(jax.random.fold_in(key, 24), (ROWS, D), jnp.float32), -6.0, 6.0)
    scales = jnp.exp(jax.random.uniform(jax.random.fold_in(key, 25), (ROWS, 1), jnp.float32, 0.0, 2.3))
    values = entries * scales
    return values.astype(jnp.bfloat16)


def setup_inputs(seed: int = 0) -> dict:
    streams_of = jax.random.split(jax.random.key(seed), 4)
    embeddings = draw_embeddings(jax.random.fold_in(streams_of[3], 71), 0)
    cluster_id = draw_cluster_id(jax.random.fold_in(streams_of[3], 71), 0)
    cluster_group = draw_cluster_group(jax.random.fold_in(streams_of[3], 71), 0)
    return dict(embeddings=embeddings, cluster_id=cluster_id, cluster_group=cluster_group)


def normalize(embeddings):
    values = embeddings.astype(jnp.float32)
    scale = lax.rsqrt(lax.optimization_barrier(jnp.sum(values * values, axis=-1, keepdims=True)) + 1e-06)
    return (values * scale).astype(jnp.bfloat16)

def reference(embeddings, cluster_id, cluster_group):
    unit = normalize(embeddings)
    dest = cluster_group[cluster_id].astype(jnp.int32)
    index = jnp.arange(ROWS, dtype=jnp.int32)
    device = index // ROWS_DEV
    local = index % ROWS_DEV
    rank = device % N_GRP * (N_CLU * ROWS_DEV) + device // N_GRP * ROWS_DEV + local
    order = jnp.argsort(dest * ROWS + rank).astype(jnp.int32)
    window = N_GRP * N_CLU * GROUP_ROW_LIMIT
    sorted_units = jnp.concatenate([jnp.zeros((window, D), jnp.float32), unit[order].astype(jnp.float32)], axis=0)
    sorted_clusters = jnp.concatenate([jnp.full((window,), -1, jnp.int32), cluster_id[order].astype(jnp.int32)], axis=0)
    sorted_groups = jnp.concatenate([jnp.full((window,), -1, jnp.int32), dest[order].astype(jnp.int32)], axis=0)
    width_q = 512

    def one_block(start):
        queries = lax.dynamic_slice_in_dim(sorted_units, start + window, width_q, 0)
        query_cl = lax.dynamic_slice_in_dim(sorted_clusters, start + window, width_q, 0)
        query_gr = lax.dynamic_slice_in_dim(sorted_groups, start + window, width_q, 0)
        keys = lax.dynamic_slice_in_dim(sorted_units, start, window + width_q, 0)
        key_cl = lax.dynamic_slice_in_dim(sorted_clusters, start, window + width_q, 0)
        key_gr = lax.dynamic_slice_in_dim(sorted_groups, start, window + width_q, 0)
        sims = jnp.dot(queries, keys.T, precision=lax.Precision.HIGHEST)
        score = jnp.where(query_cl[:, None] == key_cl[None, :], sims, 0.5 * sims)
        query_pos = jnp.arange(width_q, dtype=jnp.int32) + window
        key_pos = jnp.arange(window + width_q, dtype=jnp.int32)
        mask = (query_gr[:, None] == key_gr[None, :]) & (key_pos[None, :] < query_pos[:, None])
        return lax.optimization_barrier(jnp.max(jnp.where(mask, score, -1.0), axis=1))
    starts = jnp.arange(ROWS // width_q, dtype=jnp.int32) * width_q
    best = lax.map(one_block, starts).reshape(ROWS)
    return jnp.zeros((ROWS,), best.dtype).at[order].set(best)
```

```python
import functools

import jax
import jax.numpy as jnp
from jax import lax
from jax.experimental import pallas as pl
from jax.experimental.pallas import tpu as pltpu
from jax.sharding import PartitionSpec as P

MESH = pl.DeviceIdType.MESH
NX, NY, NZ, NC = 4, 4, 16, 2
R, D = 128, 512
NEAR = 4
NEAR_SLOTS = 2 * NEAR + 1
FAR_SLOTS = NZ - NEAR_SLOTS
PLANE = NX * NY * NC
TILE = 4 * R
NT = (((1,), (1,)), ((), ()))


def kernel(
    emb_ref, cid_ref, table_ref, out_ref,
    kb, qb, km, qm, qcl, qgr, kcl, kgr, acc_near, acc_far,
    near_out, near_in, far_out, far_in,
    zs, zr, zms, zmr, qs, qr, qms, qmr, ds, dr, dms, dmr, ns, nr, fs, fr,
):
    clu, grp = lax.axis_index("clu"), lax.axis_index("grp")
    x, z = clu // NZ, clu % NZ
    y, c = grp // NC, grp % NC
    row = y * NC + c
    me = row * NX + x

    def dev(dx=0, dy=0, dz=0, flip=False):
        xx, yy, zz = (x + dx) % NX, (y + dy) % NY, (z + dz) % NZ
        cc = 1 - c if flip else c
        return (xx * NZ + zz, yy * NC + cc)

    def slot(dx, dy, flip=False):
        cc = 1 - c if flip else c
        return (((y + dy) % NY) * NC + cc) * NX + (x + dx) % NX

    barrier = pltpu.get_barrier_semaphore()
    for step in (dict(dx=1), dict(dx=-1), dict(dy=1), dict(dy=-1), dict(dz=1), dict(dz=-1), dict(flip=True)):
        pl.semaphore_signal(barrier, inc=1, device_id=dev(**step), device_id_type=MESH)

    values = emb_ref[...].astype(jnp.float32)
    scale = lax.rsqrt(jnp.sum(values * values, axis=1, keepdims=True) + 1e-06)
    unit = (values * scale).astype(jnp.bfloat16)
    kb[0] = unit
    qb[me] = unit
    eye = lax.broadcasted_iota(jnp.int32, (R, R), 0) == lax.broadcasted_iota(jnp.int32, (R, R), 1)
    sub = lax.broadcasted_iota(jnp.int32, (R, R), 0)
    ones = jnp.ones((R, R), jnp.bfloat16)

    def column(line):
        spread = jnp.where(eye, jnp.broadcast_to(line, (R, R)), 0.0).astype(jnp.bfloat16)
        return jnp.dot(spread, ones, preferred_element_type=jnp.float32)

    cid = cid_ref[...]
    group = jnp.zeros((1, R), jnp.float32)
    for h in range(2):
        part = column(table_ref[:, h * R:(h + 1) * R].astype(jnp.float32))
        group += jnp.sum(jnp.where(jnp.broadcast_to(cid, (R, R)) == sub + h * R, part, 0.0), axis=0, keepdims=True)
    cluster = cid.astype(jnp.float32)
    km[0, 0:1, :] = cluster
    km[0, 1:2, :] = group
    qm[me, 0:1, :] = cluster
    qm[me, 1:2, :] = group

    pending = []

    def rc(src, dst, s, r, where):
        return pltpu.make_async_remote_copy(
            src_ref=src, dst_ref=dst, send_sem=s, recv_sem=r, device_id=where, device_id_type=MESH)

    def go(copy):
        copy.start()
        pending.append(copy)

    half = R // 2

    def ring(d, sign, part):
        lo = part * half
        if sign > 0:
            src = 0 if d == 1 else 2 * d - 3
            dst = 2 * d - 1
        else:
            src = 0 if d == 1 else 2 * d - 2
            dst = 2 * d if d < 8 else 15
        i = (d - 1) * 4 + (0 if sign > 0 else 2) + part
        rows = pl.ds(lo, half)
        return rc(kb.at[src, rows], kb.at[dst, rows], zs.at[i], zr.at[i], dev(dz=sign))

    def ring_meta(d, sign):
        if sign > 0:
            src, dst = (0 if d == 1 else 2 * d - 3), 2 * d - 1
        else:
            src, dst = (0 if d == 1 else 2 * d - 2), 2 * d
        i = (d - 1) * 2 + (0 if sign > 0 else 1)
        return rc(km.at[src], km.at[dst], zms.at[i], zmr.at[i], dev(dz=sign))

    def has(d, sign, part):
        return d < 8 or (sign > 0) == (part == 0)

    def has_meta(d, sign):
        return d < 8 or sign > 0

    def send(d, part):
        for sign in (1, -1):
            if has(d, sign, part):
                go(ring(d, sign, part))

    def send_meta(d):
        for sign in (1, -1):
            if has_meta(d, sign):
                go(ring_meta(d, sign))

    def pump(d, part):
        for sign in (1, -1):
            if has(d, sign, part):
                ring(d, sign, part).wait_recv()
                if d < 8 and has(d + 1, sign, part):
                    go(ring(d + 1, sign, part))
        if part == 0:
            for sign in (1, -1):
                if has_meta(d, sign):
                    ring_meta(d, sign).wait_recv()
                    if d < 8 and has_meta(d + 1, sign):
                        go(ring_meta(d + 1, sign))

    def move(h, phase, other, kind):
        along_x = (h == 0) == (phase == 0)
        step = 1 if kind[-1] == "+" else -1
        lo, n = h * half, half
        off = 0
        if kind[0] == "f":
            n = half // 2
            lo += 0 if step > 0 else n
            off = -step
        if along_x:
            s = slot(off, other if phase == 1 else 0)
            target = dev(dx=step)
        else:
            s = slot(other if phase == 1 else 0, off)
            target = dev(dy=step)
        i = h * 20 + (0 if phase == 0 else 4 + 4 * (other % 4)) + ("+", "-", "f+", "f-").index(kind)
        ref = qb.at[s, pl.ds(lo, n)]
        return rc(ref, ref, qs.at[i], qr.at[i], target)

    def move_meta(phase, other, kind):
        step = -1 if kind == "-" else 1
        off = -1 if kind == "f+" else 0
        if phase == 0:
            s, target = slot(off, 0), dev(dx=step)
        else:
            s, target = slot(other, off), dev(dy=step)
        i = (0 if phase == 0 else 3 + 3 * (other % 4)) + ("+", "-", "f+").index(kind)
        return rc(qm.at[s], qm.at[s], qms.at[i], qmr.at[i], target)

    def share(dx, dy):
        s = slot(dx, dy)
        i = (dy % 4) * 4 + dx % 4
        return (rc(qb.at[s], qb.at[s], ds.at[i], dr.at[i], dev(flip=True)),
                rc(qm.at[s], qm.at[s], dms.at[i], dmr.at[i], dev(flip=True)))

    def give(dx, dy):
        for copy in share(dx, dy):
            go(copy)

    pl.semaphore_wait(barrier, 7)

    send_meta(1)
    go(move_meta(0, 0, "+"))
    go(move_meta(0, 0, "-"))
    go(move_meta(1, 0, "+"))
    go(move_meta(1, 0, "-"))
    send(1, 0)
    for h in range(2):
        go(move(h, 0, 0, "+"))
        go(move(h, 0, 0, "-"))
    send(1, 1)
    for h in range(2):
        go(move(h, 1, 0, "+"))
        go(move(h, 1, 0, "-"))
    give(0, 0)
    for sign, off in (("+", -1), ("-", 1)):
        for h in range(2):
            move(h, 0, 0, sign).wait_recv()
            go(move(h, 0, 0, "f" + sign))
        move_meta(0, 0, sign).wait_recv()
        if sign == "+":
            go(move_meta(0, 0, "f+"))
        go(move_meta(1, off, "+"))
        go(move_meta(1, off, "-"))
        for h in range(2):
            go(move(h, 1, off, "+"))
            go(move(h, 1, off, "-"))
    pump(1, 0)
    pump(1, 1)
    for sign in ("+", "-"):
        for h in range(2):
            move(h, 1, 0, sign).wait_recv()
            go(move(h, 1, 0, "f" + sign))
        move_meta(1, 0, sign).wait_recv()
        if sign == "+":
            go(move_meta(1, 0, "f+"))
    give(-1, 0)
    give(1, 0)
    give(0, -1)
    give(0, 1)
    for h in range(2):
        for sign in ("+", "-"):
            move(h, 0, 0, "f" + sign).wait_recv()
    move_meta(0, 0, "f+").wait_recv()
    go(move_meta(1, 2, "+"))
    go(move_meta(1, 2, "-"))
    for h in range(2):
        go(move(h, 1, 2, "+"))
        go(move(h, 1, 2, "-"))
    pump(2, 0)
    pump(2, 1)
    for off in (-1, 1):
        for sign in ("+", "-"):
            for h in range(2):
                move(h, 1, off, sign).wait_recv()
                go(move(h, 1, off, "f" + sign))
            move_meta(1, off, sign).wait_recv()
        go(move_meta(1, off, "f+"))
    for h in range(2):
        for sign in ("+", "-"):
            move(h, 1, 0, "f" + sign).wait_recv()
    move_meta(1, 0, "f+").wait_recv()
    for dx, dy in ((-1, -1), (-1, 1), (1, -1), (1, 1), (2, 0), (0, 2)):
        give(dx, dy)
    pump(3, 0)
    pump(3, 1)
    for sign in ("+", "-"):
        for h in range(2):
            move(h, 1, 2, sign).wait_recv()
            go(move(h, 1, 2, "f" + sign))
        move_meta(1, 2, sign).wait_recv()
    go(move_meta(1, 2, "f+"))
    for off in (-1, 1):
        for h in range(2):
            for sign in ("+", "-"):
                move(h, 1, off, "f" + sign).wait_recv()
        move_meta(1, off, "f+").wait_recv()
    for dx, dy in ((2, -1), (2, 1), (-1, 2), (1, 2)):
        give(dx, dy)
    for h in range(2):
        for sign in ("+", "-"):
            move(h, 1, 2, "f" + sign).wait_recv()
    move_meta(1, 2, "f+").wait_recv()
    give(2, 2)
    pump(4, 0)
    for dy in range(NY):
        for dx in range(NX):
            for copy in share(dx, dy):
                copy.wait_recv()

    acc_near[...] = jnp.full(acc_near.shape, -1.0, jnp.float32)
    acc_far[...] = jnp.full(acc_far.shape, -1.0, jnp.float32)

    def q_columns(s, carry):
        rows = pl.ds(pl.multiple_of(s * R, R), R)
        qcl[rows, :] = column(qm[s, 0:1, :])
        qgr[rows, :] = jnp.where(s < me, column(qm[s, 1:2, :]), -1.0)
        return carry

    lax.fori_loop(0, PLANE, q_columns, 0)

    def tile(stream, lanes, s_cl, s_gr, l_cl, l_gr, acc, at):
        sims = lax.dot_general(stream, lanes, NT, preferred_element_type=jnp.float32)
        n = sims.shape[0] // 8
        for j in range(sims.shape[1] // R):
            s = sims[:, j * R:(j + 1) * R]
            score = jnp.where(s_cl == l_cl[j], s, 0.5 * s)
            gr = s_gr[j] if isinstance(s_gr, list) else s_gr
            score = jnp.where(gr == l_gr[j], score, -1.0)
            best = jnp.max(score.reshape(n, 8, R), axis=0)
            where = pl.ds(pl.multiple_of(at + j * R, R), R)
            acc[:, where] = jnp.maximum(acc[:, where], best)

    def lines(ref, s, n, ok=None):
        cl = [ref[s + j, 0:1, :] for j in range(n)]
        gr = [ref[s + j, 1:2, :] for j in range(n)]
        return cl, gr

    def near(t, first, n):
        rows = pl.ds(pl.multiple_of(t * TILE, TILE), TILE)
        stream = qb[pl.ds(t * 4, 4)].reshape(TILE, D)
        cl, gr = lines(km, first, n)
        lanes = kb[first:first + n].reshape(n * R, D)
        tile(stream, lanes, qcl[rows, :], qgr[rows, :], cl, gr, acc_near, first * R)

    def k_columns(s):
        rows = pl.ds((s - NEAR_SLOTS) * R, R)
        kcl[rows, :] = column(km[s, 0:1, :])
        kgr[rows, :] = column(km[s, 1:2, :])

    def far(t, first, n, wide):
        rows = pl.ds((first - NEAR_SLOTS) * R, n * R)
        stream = kb[first:first + n].reshape(n * R, D)
        lanes = qb[pl.ds(t * 4, wide)].reshape(wide * R, D)
        cl, gr = lines(qm, t * 4, wide)
        gr = [jnp.where(t * 4 + j > me, g, -2.0) for j, g in enumerate(gr)]
        tile(stream, lanes, kcl[rows, :], kgr[rows, :], cl, gr, acc_far, t * TILE)

    def origin(s):
        if s == 0:
            return z
        d = (s + 1) // 2
        return (z - d) % NZ if s % 2 else (z + d) % NZ

    def own_near():
        stream = kb[0]
        cl, gr = lines(km, 0, NEAR_SLOTS)
        s_cl, s_gr = column(cl[0]), column(gr[0])
        lane = lax.broadcasted_iota(jnp.int32, (R, R), 1)
        groups = [jnp.where(sub < lane, s_gr, -1.0)]
        for s in range(1, NEAR_SLOTS):
            groups.append(jnp.where(origin(s) > z, s_gr, -1.0))
        tile(stream, kb[0:NEAR_SLOTS].reshape(NEAR_SLOTS * R, D), s_cl, groups, cl, gr, acc_near, 0)

    def own_far(first, n):
        stream = kb[first:first + n].reshape(n * R, D)
        rows = pl.ds((first - NEAR_SLOTS) * R, n * R)
        groups = jnp.concatenate(
            [jnp.where(origin(first + j) < z, kgr[pl.ds((first + j - NEAR_SLOTS) * R, R), :], -1.0) for j in range(n)], axis=0)
        tile(stream, kb[0], kcl[rows, :], groups, [km[0, 0:1, :]], [km[0, 1:2, :]], acc_far, me * R)

    def near_if(t):
        @pl.when(t * 4 < me)
        def _():
            near(t, 0, NEAR_SLOTS)

    def far_loop(first, n):
        def body(t, carry):
            far(t, first, n, 4)
            return carry
        lax.fori_loop((me + 1) // 4, PLANE // 4, body, 0)

    pump(4, 1)
    own_near()
    near_if(0)
    pump(5, 0)
    near_if(1)
    pump(5, 1)
    near_if(2)
    near_if(3)
    pump(6, 0)
    k_columns(9)
    k_columns(10)
    far_loop(9, 2)
    near_if(4)
    pump(6, 1)
    near_if(5)
    pump(7, 0)
    k_columns(11)
    k_columns(12)
    far_loop(11, 2)
    near_if(6)
    pump(7, 1)
    near_if(7)

    def back(s):
        d = (s + 1) // 2
        step, other = (-d, 2 * d) if s % 2 else (d, 2 * d - 1)
        return rc(near_out.at[s], near_in.at[other], ns.at[s], nr.at[s], dev(dz=step))

    for s in range(NEAR_SLOTS):
        near_out[s] = jnp.max(acc_near[:, s * R:(s + 1) * R], axis=0, keepdims=True)
    for s in range(1, NEAR_SLOTS):
        go(back(s))
    k_columns(13)
    k_columns(14)
    far_loop(13, 2)
    pump(8, 0)
    pump(8, 1)
    k_columns(15)
    far_loop(15, 1)
    own_far(NEAR_SLOTS, FAR_SLOTS)

    for s in range(PLANE):
        far_out[s] = jnp.max(acc_far[:, s * R:(s + 1) * R], axis=0, keepdims=True)

    def reply(k):
        dx, dy, flip = k % NX, (k // NX) % NY, k >= NX * NY
        return rc(far_out.at[slot(dx, dy, flip)], far_in.at[k], fs.at[k], fr.at[k], dev(dx, dy, 0, flip))

    for k in range(1, PLANE):
        go(reply(k))
    best = jnp.maximum(near_out[0], far_out[me])
    for s in range(1, NEAR_SLOTS):
        back(s).wait_recv()
    for s in range(1, NEAR_SLOTS):
        best = jnp.maximum(best, near_in[s])
    for k in range(1, PLANE):
        reply(k).wait_recv()
    for k in range(1, PLANE):
        best = jnp.maximum(best, far_in[k])
    out_ref[...] = best
    for copy in pending:
        copy.wait_send()


def solution(mesh):
    def step(embeddings, cluster_id, cluster_group):
        dma = pltpu.SemaphoreType.DMA
        f32 = jnp.float32
        best = pl.pallas_call(
            kernel,
            out_shape=jax.ShapeDtypeStruct((1, R), f32),
            in_specs=[pl.BlockSpec(memory_space=pltpu.VMEM)] * 3,
            out_specs=pl.BlockSpec(memory_space=pltpu.VMEM),
            scratch_shapes=[
                pltpu.VMEM((NZ, R, D), jnp.bfloat16),
                pltpu.VMEM((PLANE, R, D), jnp.bfloat16),
                pltpu.VMEM((NZ, 2, R), f32),
                pltpu.VMEM((PLANE, 2, R), f32),
                pltpu.VMEM((PLANE * R, R), f32),
                pltpu.VMEM((PLANE * R, R), f32),
                pltpu.VMEM((FAR_SLOTS * R, R), f32),
                pltpu.VMEM((FAR_SLOTS * R, R), f32),
                pltpu.VMEM((8, NEAR_SLOTS * R), f32),
                pltpu.VMEM((8, PLANE * R), f32),
                pltpu.VMEM((NEAR_SLOTS, 1, R), f32),
                pltpu.VMEM((NEAR_SLOTS, 1, R), f32),
                pltpu.VMEM((PLANE, 1, R), f32),
                pltpu.VMEM((PLANE, 1, R), f32),
                dma((32,)), dma((32,)), dma((16,)), dma((16,)),
                dma((40,)), dma((40,)), dma((15,)), dma((15,)),
                dma((16,)), dma((16,)), dma((16,)), dma((16,)),
                dma((NEAR_SLOTS,)), dma((NEAR_SLOTS,)), dma((PLANE,)), dma((PLANE,)),
            ],
            compiler_params=pltpu.CompilerParams(
                collective_id=0, has_side_effects=True, vmem_limit_bytes=60 * 2**20),
        )(embeddings, cluster_id.reshape(1, R), cluster_group.reshape(1, -1))
        return best.reshape(R)

    placed = (P(("clu", "grp"), None), P(("clu", "grp")), P())
    return jax.shard_map(step, mesh=mesh, in_specs=placed, out_specs=P(("clu", "grp")), check_vma=False)
```

```python
import functools

import jax
import jax.numpy as jnp
from jax import lax
from jax.experimental import pallas as pl
from jax.experimental.pallas import tpu as pltpu
from jax.sharding import PartitionSpec as P

MESH = pl.DeviceIdType.MESH
NX, NY, NZ, NC = 4, 4, 16, 2
R, D = 128, 512
NEAR = 4
NEAR_SLOTS = 2 * NEAR + 1
PLANE = NX * NY * NC
TILE = 4 * R
NT = (((1,), (1,)), ((), ()))


def kernel(
    emb_ref, cid_ref, table_ref, out_ref,
    kb, qb, km, qm, kcl, kgr, acc_near, acc_far,
    near_out, near_in, far_out, far_in,
    zs, zr, zms, zmr, qs, qr, qms, qmr, ds, dr, dms, dmr, ns, nr, fs, fr,
):
    clu, grp = lax.axis_index("clu"), lax.axis_index("grp")
    x, z = clu // NZ, clu % NZ
    y, c = grp // NC, grp % NC
    row = y * NC + c
    me = row * NX + x

    def dev(dx=0, dy=0, dz=0, flip=False):
        xx, yy, zz = (x + dx) & 3, (y + dy) & 3, (z + dz) & 15
        cc = 1 - c if flip else c
        return (xx * NZ + zz, yy * NC + cc)

    def slot(dx, dy, flip=False):
        cc = 1 - c if flip else c
        return (((y + dy) & 3) * NC + cc) * NX + ((x + dx) & 3)

    barrier = pltpu.get_barrier_semaphore()
    for step in (dict(dx=1), dict(dx=-1), dict(dy=1), dict(dy=-1), dict(dz=1), dict(dz=-1), dict(flip=True)):
        pl.semaphore_signal(barrier, inc=1, device_id=dev(**step), device_id_type=MESH)

    values = emb_ref[...].astype(jnp.float32)
    scale = lax.rsqrt(jnp.sum(values * values, axis=1, keepdims=True) + 1e-06)
    unit = (values * scale).astype(jnp.bfloat16)
    kb[0] = unit
    qb[me] = unit
    eye = lax.broadcasted_iota(jnp.int32, (R, R), 0) == lax.broadcasted_iota(jnp.int32, (R, R), 1)
    sub = lax.broadcasted_iota(jnp.int32, (R, R), 0)
    ones = jnp.ones((R, R), jnp.bfloat16)

    def column(line):
        spread = jnp.where(eye, jnp.broadcast_to(line, (R, R)), 0.0).astype(jnp.bfloat16)
        return jnp.dot(spread, ones, preferred_element_type=jnp.float32)

    cid = cid_ref[...]
    group = jnp.zeros((1, R), jnp.float32)
    for h in range(2):
        part = column(table_ref[:, h * R:(h + 1) * R].astype(jnp.float32))
        group += jnp.sum(jnp.where(jnp.broadcast_to(cid, (R, R)) == sub + h * R, part, 0.0), axis=0, keepdims=True)
    cluster = cid.astype(jnp.float32)
    km[0, 0:1, :] = cluster
    km[0, 1:2, :] = group
    qm[me, 0:1, :] = cluster
    qm[me, 1:2, :] = group

    pending = []

    def rc(src, dst, s, r, where):
        return pltpu.make_async_remote_copy(
            src_ref=src, dst_ref=dst, send_sem=s, recv_sem=r, device_id=where, device_id_type=MESH)

    def go(copy):
        copy.start()
        pending.append(copy)

    half = R // 2

    def ring(d, sign):
        if sign > 0:
            src, dst, lo = (0 if d == 1 else 2 * d - 3), 2 * d - 1, 0
        else:
            src, dst, lo = (0 if d == 1 else 2 * d - 2), min(2 * d, 15), half
        i = (d - 1) * 2 + (0 if sign > 0 else 1)
        rows = pl.ds(lo, half) if d == 8 else pl.ds(0, R)
        return rc(kb.at[src, rows], kb.at[dst, rows], zs.at[i], zr.at[i], dev(dz=sign))

    def ring_meta(d, sign):
        if sign > 0:
            src, dst = (0 if d == 1 else 2 * d - 3), 2 * d - 1
        else:
            src, dst = (0 if d == 1 else 2 * d - 2), 2 * d
        i = (d - 1) * 2 + (0 if sign > 0 else 1)
        return rc(km.at[src], km.at[dst], zms.at[i], zmr.at[i], dev(dz=sign))

    def forward(d):
        for sign in (1, -1):
            go(ring(d, sign))
        for sign in (1, -1) if d < 8 else (1,):
            go(ring_meta(d, sign))

    def pump(d):
        for sign in (1, -1):
            ring(d, sign).wait_recv()
            if d < 8:
                go(ring(d + 1, sign))
        for sign in (1, -1) if d < 8 else (1,):
            ring_meta(d, sign).wait_recv()
            if d < 7 or (d == 7 and sign > 0):
                go(ring_meta(d + 1, sign))

    def move(h, phase, other, kind):
        along_x = (h == 0) == (phase == 0)
        step = 1 if kind[-1] == "+" else -1
        lo, n = h * half, half
        off = 0
        if kind[0] == "f":
            n = half // 2
            lo += 0 if step > 0 else n
            off = -step
        if along_x:
            s = slot(off, other if phase == 1 else 0)
            target = dev(dx=step)
        else:
            s = slot(other if phase == 1 else 0, off)
            target = dev(dy=step)
        i = h * 20 + (0 if phase == 0 else 4 + 4 * (other % 4)) + ("+", "-", "f+", "f-").index(kind)
        ref = qb.at[s, pl.ds(lo, n)]
        return rc(ref, ref, qs.at[i], qr.at[i], target)

    def move_meta(phase, other, kind):
        step = -1 if kind == "-" else 1
        off = -1 if kind == "f+" else 0
        if phase == 0:
            s, target = slot(off, 0), dev(dx=step)
        else:
            s, target = slot(other, off), dev(dy=step)
        i = (0 if phase == 0 else 3 + 3 * (other % 4)) + ("+", "-", "f+").index(kind)
        return rc(qm.at[s], qm.at[s], qms.at[i], qmr.at[i], target)

    def share(dx, dy):
        s = slot(dx, dy)
        i = (dy % 4) * 4 + dx % 4
        return (rc(qb.at[s], qb.at[s], ds.at[i], dr.at[i], dev(flip=True)),
                rc(qm.at[s], qm.at[s], dms.at[i], dmr.at[i], dev(flip=True)))

    def give(dx, dy):
        for copy in share(dx, dy):
            go(copy)

    pl.semaphore_wait(barrier, 7)

    forward(1)
    go(move_meta(0, 0, "+"))
    go(move_meta(0, 0, "-"))
    go(move_meta(1, 0, "+"))
    go(move_meta(1, 0, "-"))
    for h in range(2):
        go(move(h, 0, 0, "+"))
        go(move(h, 0, 0, "-"))
    for h in range(2):
        go(move(h, 1, 0, "+"))
        go(move(h, 1, 0, "-"))
    give(0, 0)
    for sign, off in (("+", -1), ("-", 1)):
        for h in range(2):
            move(h, 0, 0, sign).wait_recv()
            go(move(h, 0, 0, "f" + sign))
        move_meta(0, 0, sign).wait_recv()
        if sign == "+":
            go(move_meta(0, 0, "f+"))
        go(move_meta(1, off, "+"))
        go(move_meta(1, off, "-"))
        for h in range(2):
            go(move(h, 1, off, "+"))
            go(move(h, 1, off, "-"))
    pump(1)
    for sign in ("+", "-"):
        for h in range(2):
            move(h, 1, 0, sign).wait_recv()
            go(move(h, 1, 0, "f" + sign))
        move_meta(1, 0, sign).wait_recv()
        if sign == "+":
            go(move_meta(1, 0, "f+"))
    give(-1, 0)
    give(1, 0)
    give(0, -1)
    give(0, 1)
    for h in range(2):
        for sign in ("+", "-"):
            move(h, 0, 0, "f" + sign).wait_recv()
    move_meta(0, 0, "f+").wait_recv()
    go(move_meta(1, 2, "+"))
    go(move_meta(1, 2, "-"))
    for h in range(2):
        go(move(h, 1, 2, "+"))
        go(move(h, 1, 2, "-"))
    pump(2)
    for off in (-1, 1):
        for sign in ("+", "-"):
            for h in range(2):
                move(h, 1, off, sign).wait_recv()
                go(move(h, 1, off, "f" + sign))
            move_meta(1, off, sign).wait_recv()
        go(move_meta(1, off, "f+"))
    for h in range(2):
        for sign in ("+", "-"):
            move(h, 1, 0, "f" + sign).wait_recv()
    move_meta(1, 0, "f+").wait_recv()
    for dx, dy in ((-1, -1), (-1, 1), (1, -1), (1, 1), (2, 0), (0, 2)):
        give(dx, dy)
    pump(3)
    for sign in ("+", "-"):
        for h in range(2):
            move(h, 1, 2, sign).wait_recv()
            go(move(h, 1, 2, "f" + sign))
        move_meta(1, 2, sign).wait_recv()
    go(move_meta(1, 2, "f+"))
    for off in (-1, 1):
        for h in range(2):
            for sign in ("+", "-"):
                move(h, 1, off, "f" + sign).wait_recv()
        move_meta(1, off, "f+").wait_recv()
    for dx, dy in ((2, -1), (2, 1), (-1, 2), (1, 2)):
        give(dx, dy)
    for h in range(2):
        for sign in ("+", "-"):
            move(h, 1, 2, "f" + sign).wait_recv()
    move_meta(1, 2, "f+").wait_recv()
    give(2, 2)
    pump(4)
    acc_near[...] = jnp.full(acc_near.shape, -1.0, jnp.float32)
    acc_far[...] = jnp.full(acc_far.shape, -1.0, jnp.float32)

    def k_columns(first, n):
        for s in range(first, first + n):
            rows = pl.ds(s * R, R)
            kcl[rows, :] = column(km[s, 0:1, :])
            kgr[rows, :] = column(km[s, 1:2, :])

    def scores(sims, j, s_cl, s_gr, l_cl, l_gr):
        s = sims[:, j * R:(j + 1) * R]
        score = jnp.where(s_cl == l_cl, s, 0.5 * s)
        return jnp.where(s_gr == l_gr, score, -1.0)

    def near(t):
        stream = kb[0:NEAR_SLOTS].reshape(NEAR_SLOTS * R, D)
        lanes = qb[pl.ds(t * 4, 4)].reshape(TILE, D)
        sims = lax.dot_general(stream, lanes, NT, preferred_element_type=jnp.float32)
        rows = pl.ds(0, NEAR_SLOTS * R)
        best = acc_near[...]
        for j in range(4):
            q = t * 4 + j
            gr = jnp.where(q < me, qm[q, 1:2, :], -2.0)
            best = jnp.maximum(best, scores(sims, j, kcl[rows, :], kgr[rows, :], qm[q, 0:1, :], gr))
        acc_near[...] = best

    def near_loop(lo, hi):
        def body(t, carry):
            near(t)
            return carry
        lax.fori_loop(lo, hi, body, 0)

    def origin(s):
        if s == 0:
            return z
        d = (s + 1) // 2
        return (z - d) & 15 if s % 2 else (z + d) & 15

    def own_near():
        stream = kb[0:NEAR_SLOTS].reshape(NEAR_SLOTS * R, D)
        sims = lax.dot_general(stream, kb[0], NT, preferred_element_type=jnp.float32)
        rows = pl.ds(0, NEAR_SLOTS * R)
        lane = lax.broadcasted_iota(jnp.int32, (R, R), 1)
        groups = [jnp.where(sub > lane, kgr[0:R, :], -1.0)]
        for s in range(1, NEAR_SLOTS):
            groups.append(jnp.where(origin(s) > z, kgr[s * R:(s + 1) * R, :], -1.0))
        acc_near[...] = jnp.maximum(acc_near[...], scores(
            sims, 0, kcl[rows, :], jnp.concatenate(groups, axis=0), km[0, 0:1, :], km[0, 1:2, :]))

    def into_far(best, s):
        where = pl.ds(pl.multiple_of(s * R, R), R)
        n = best.shape[0] // 8
        acc_far[:, where] = jnp.maximum(acc_far[:, where], jnp.max(best.reshape(n, 8, R), axis=0))

    def far(t, first, n):
        rows = pl.ds(first * R, n * R)
        stream = kb[first:first + n].reshape(n * R, D)
        lanes = qb[pl.ds(t * 8, 8)].reshape(2 * TILE, D)
        sims = lax.dot_general(stream, lanes, NT, preferred_element_type=jnp.float32)
        for j in range(8):
            q = t * 8 + j
            later = q > me
            if n == 1:
                later = later | ((q == me) & (origin(first) < z))
            gr = jnp.where(later, qm[q, 1:2, :], -2.0)
            into_far(scores(sims, j, kcl[rows, :], kgr[rows, :], qm[q, 0:1, :], gr), q)

    def far_loop(first, n):
        def body(t, carry):
            far(t, first, n)
            return carry
        lax.fori_loop(me // 8, PLANE // 8, body, 0)

    def own_far(first, n):
        stream = kb[first:first + n].reshape(n * R, D)
        sims = lax.dot_general(stream, kb[0], NT, preferred_element_type=jnp.float32)
        groups = jnp.concatenate(
            [jnp.where(origin(s) < z, kgr[s * R:(s + 1) * R, :], -1.0) for s in range(first, first + n)], axis=0)
        into_far(scores(sims, 0, kcl[pl.ds(first * R, n * R), :], groups, km[0, 0:1, :], km[0, 1:2, :]), me)

    k_columns(0, NEAR_SLOTS)
    own_near()
    for dy in range(NY):
        for dx in range(NX):
            for copy in share(dx, dy):
                copy.wait_recv()
    rest = jnp.maximum(row - 1, 0)
    near_a = jnp.minimum(row + 1, 2)
    near_b = near_a + (rest + 2) // 3
    near_c = near_b + (rest + 1) // 3
    near_loop(0, near_a)
    pump(5)
    k_columns(9, 2)
    far_loop(9, 2)
    near_loop(near_a, near_b)
    pump(6)
    k_columns(11, 2)
    far_loop(11, 2)
    near_loop(near_b, near_c)
    pump(7)
    k_columns(13, 2)
    far_loop(13, 2)
    near_loop(near_c, row + 1)
    own_far(9, 6)

    def back(s):
        d = (s + 1) // 2
        step, other = (-d, 2 * d) if s % 2 else (d, 2 * d - 1)
        return rc(near_out.at[s], near_in.at[other], ns.at[s], nr.at[s], dev(dz=step))

    for s in range(NEAR_SLOTS):
        near_out[s] = jnp.max(acc_near[s * R:(s + 1) * R, :].T, axis=0, keepdims=True)
    for s in range(1, NEAR_SLOTS):
        go(back(s))
    pump(8)
    k_columns(15, 1)
    far_loop(15, 1)

    for s in range(PLANE):
        far_out[s] = jnp.max(acc_far[:, s * R:(s + 1) * R], axis=0, keepdims=True)

    def reply(k):
        dx, dy, flip = k % NX, (k // NX) % NY, k >= NX * NY
        return rc(far_out.at[slot(dx, dy, flip)], far_in.at[k], fs.at[k], fr.at[k], dev(dx, dy, 0, flip))

    for k in range(1, PLANE):
        go(reply(k))
    best = jnp.maximum(near_out[0], far_out[me])
    for s in range(1, NEAR_SLOTS):
        back(s).wait_recv()
    for s in range(1, NEAR_SLOTS):
        best = jnp.maximum(best, near_in[s])
    for k in range(1, PLANE):
        reply(k).wait_recv()
    for k in range(1, PLANE):
        best = jnp.maximum(best, far_in[k])
    out_ref[...] = best
    for copy in pending:
        copy.wait_send()


def solution(mesh):
    def step(embeddings, cluster_id, cluster_group):
        dma = pltpu.SemaphoreType.DMA
        f32 = jnp.float32
        best = pl.pallas_call(
            kernel,
            out_shape=jax.ShapeDtypeStruct((1, R), f32),
            in_specs=[pl.BlockSpec(memory_space=pltpu.VMEM)] * 3,
            out_specs=pl.BlockSpec(memory_space=pltpu.VMEM),
            scratch_shapes=[
                pltpu.VMEM((NZ, R, D), jnp.bfloat16),
                pltpu.VMEM((PLANE, R, D), jnp.bfloat16),
                pltpu.VMEM((NZ, 2, R), f32),
                pltpu.VMEM((PLANE, 2, R), f32),
                pltpu.VMEM((NZ * R, R), f32),
                pltpu.VMEM((NZ * R, R), f32),
                pltpu.VMEM((NEAR_SLOTS * R, R), f32),
                pltpu.VMEM((8, PLANE * R), f32),
                pltpu.VMEM((NEAR_SLOTS, 1, R), f32),
                pltpu.VMEM((NEAR_SLOTS, 1, R), f32),
                pltpu.VMEM((PLANE, 1, R), f32),
                pltpu.VMEM((PLANE, 1, R), f32),
                dma((16,)), dma((16,)), dma((16,)), dma((16,)),
                dma((40,)), dma((40,)), dma((15,)), dma((15,)),
                dma((16,)), dma((16,)), dma((16,)), dma((16,)),
                dma((NEAR_SLOTS,)), dma((NEAR_SLOTS,)), dma((PLANE,)), dma((PLANE,)),
            ],
            compiler_params=pltpu.CompilerParams(
                collective_id=0, has_side_effects=True, vmem_limit_bytes=60 * 2**20),
        )(embeddings, cluster_id.reshape(1, R), cluster_group.reshape(1, -1))
        return best.reshape(R)

    placed = (P(("clu", "grp"), None), P(("clu", "grp")), P())
    return jax.shard_map(step, mesh=mesh, in_specs=placed, out_specs=P(("clu", "grp")), check_vma=False)
```

```python
import functools

import jax
import jax.numpy as jnp
from jax import lax
from jax.experimental import pallas as pl
from jax.experimental.pallas import tpu as pltpu
from jax.sharding import PartitionSpec as P

MESH = pl.DeviceIdType.MESH
NX, NY, NZ, NC = 4, 4, 16, 2
R, D = 128, 512
NEAR = 4
NEAR_SLOTS = 2 * NEAR + 1
PLANE = NX * NY * NC
TILE = 4 * R
NT = (((1,), (1,)), ((), ()))
CHUNKS = (0, 4, 4, 4, 4, 4, 1, 1, 1)
START = tuple(2 * sum(CHUNKS[:d]) for d in range(NZ // 2 + 1))


def kernel(
    emb_ref, cid_ref, table_ref, out_ref,
    kb, qb, km, qm, kcl, kgr, acc_near, acc_far,
    near_out, near_in, far_out, far_in,
    zs, zr, zms, zmr, qs, qr, qms, qmr, ds, dr, dms, dmr, ns, nr, fs, fr,
):
    clu, grp = lax.axis_index("clu"), lax.axis_index("grp")
    x, z = clu // NZ, clu % NZ
    y, c = grp // NC, grp % NC
    row = y * NC + c
    me = row * NX + x

    def dev(dx=0, dy=0, dz=0, flip=False):
        xx, yy, zz = (x + dx) & 3, (y + dy) & 3, (z + dz) & 15
        cc = 1 - c if flip else c
        return (xx * NZ + zz, yy * NC + cc)

    def slot(dx, dy, flip=False):
        cc = 1 - c if flip else c
        return (((y + dy) & 3) * NC + cc) * NX + ((x + dx) & 3)

    barrier = pltpu.get_barrier_semaphore()
    for step in (dict(dx=1), dict(dx=-1), dict(dy=1), dict(dy=-1), dict(dz=1), dict(dz=-1), dict(flip=True)):
        pl.semaphore_signal(barrier, inc=1, device_id=dev(**step), device_id_type=MESH)

    values = emb_ref[...].astype(jnp.float32)
    scale = lax.rsqrt(jnp.sum(values * values, axis=1, keepdims=True) + 1e-06)
    unit = (values * scale).astype(jnp.bfloat16)
    kb[0] = unit
    qb[me] = unit
    eye = lax.broadcasted_iota(jnp.int32, (R, R), 0) == lax.broadcasted_iota(jnp.int32, (R, R), 1)
    sub = lax.broadcasted_iota(jnp.int32, (R, R), 0)
    ones = jnp.ones((R, R), jnp.bfloat16)

    def column(line):
        spread = jnp.where(eye, jnp.broadcast_to(line, (R, R)), 0.0).astype(jnp.bfloat16)
        return jnp.dot(spread, ones, preferred_element_type=jnp.float32)

    cid = cid_ref[...]
    group = jnp.zeros((1, R), jnp.float32)
    for h in range(2):
        part = column(table_ref[:, h * R:(h + 1) * R].astype(jnp.float32))
        group += jnp.sum(jnp.where(jnp.broadcast_to(cid, (R, R)) == sub + h * R, part, 0.0), axis=0, keepdims=True)
    cluster = cid.astype(jnp.float32)
    km[0, 0:1, :] = cluster
    km[0, 1:2, :] = group
    qm[me, 0:1, :] = cluster
    qm[me, 1:2, :] = group

    pending = []

    def rc(src, dst, s, r, where):
        return pltpu.make_async_remote_copy(
            src_ref=src, dst_ref=dst, send_sem=s, recv_sem=r, device_id=where, device_id_type=MESH)

    def go(copy):
        copy.start()
        pending.append(copy)

    half = R // 2
    way = 1 - 2 * c
    twin = slot(0, 0, True)

    def ring(d, o, part):
        n = R // CHUNKS[d]
        rows = pl.ds(part * n, n)
        if d == 1:
            src = kb.at[0, rows] if o == 0 else qb.at[twin, rows]
        else:
            src = kb.at[2 * d - 3 + o, rows]
        i = START[d] + o * CHUNKS[d] + part
        return rc(src, kb.at[2 * d - 1 + o, rows], zs.at[i], zr.at[i], dev(dz=way))

    def ring_meta(d, o):
        if d == 1:
            src = km.at[0] if o == 0 else qm.at[twin]
        else:
            src = km.at[2 * d - 3 + o]
        i = 2 * d - 1 + o
        return rc(src, km.at[i], zms.at[i], zmr.at[i], dev(dz=way))

    def forward(d, o, lo, hi):
        for part in range(CHUNKS[d]):
            if lo < (part + 1) * (R // CHUNKS[d]) <= hi:
                go(ring(d, o, part))

    def pump(d, o):
        ring_meta(d, o).wait_recv()
        more = d < 7 or (d == 7 and o == 0)
        if more:
            go(ring_meta(d + 1, o))
        n = R // CHUNKS[d]
        for part in range(CHUNKS[d]):
            ring(d, o, part).wait_recv()
            if more:
                forward(d + 1, o, part * n, (part + 1) * n)

    def move(h, phase, other, kind):
        along_x = (h == 0) == (phase == 0)
        step = 1 if kind[-1] == "+" else -1
        lo, n = h * half, half
        off = 0
        if kind[0] == "f":
            n = half // 2
            lo += 0 if step > 0 else n
            off = -step
        if along_x:
            s = slot(off, other if phase == 1 else 0)
            target = dev(dx=step)
        else:
            s = slot(other if phase == 1 else 0, off)
            target = dev(dy=step)
        i = h * 20 + (0 if phase == 0 else 4 + 4 * (other % 4)) + ("+", "-", "f+", "f-").index(kind)
        ref = qb.at[s, pl.ds(lo, n)]
        return rc(ref, ref, qs.at[i], qr.at[i], target)

    def move_meta(phase, other, kind):
        step = -1 if kind == "-" else 1
        off = -1 if kind == "f+" else 0
        if phase == 0:
            s, target = slot(off, 0), dev(dx=step)
        else:
            s, target = slot(other, off), dev(dy=step)
        i = (0 if phase == 0 else 3 + 3 * (other % 4)) + ("+", "-", "f+").index(kind)
        return rc(qm.at[s], qm.at[s], qms.at[i], qmr.at[i], target)

    def share(dx, dy):
        s = slot(dx, dy)
        i = (dy % 4) * 4 + dx % 4
        return (rc(qb.at[s], qb.at[s], ds.at[i], dr.at[i], dev(flip=True)),
                rc(qm.at[s], qm.at[s], dms.at[i], dmr.at[i], dev(flip=True)))

    def give(dx, dy):
        for copy in share(dx, dy):
            go(copy)

    pl.semaphore_wait(barrier, 7)

    def line(off):
        sign = "+" if off < 0 else "-"
        for h in range(2):
            move(h, 0, 0, sign).wait_recv()
            go(move(h, 0, 0, "f" + sign))
        move_meta(0, 0, sign).wait_recv()
        if sign == "+":
            go(move_meta(0, 0, "f+"))
        go(move_meta(1, off, "+"))
        go(move_meta(1, off, "-"))
        for h in range(2):
            go(move(h, 1, off, "+"))
            go(move(h, 1, off, "-"))

    def cross(off):
        for sign in ("+", "-"):
            for h in range(2):
                move(h, 1, off, sign).wait_recv()
                go(move(h, 1, off, "f" + sign))
            move_meta(1, off, sign).wait_recv()
        go(move_meta(1, off, "f+"))

    def cross_end(off):
        for h in range(2):
            for sign in ("+", "-"):
                move(h, 1, off, "f" + sign).wait_recv()
        move_meta(1, off, "f+").wait_recv()

    go(ring_meta(1, 0))
    give(0, 0)
    forward(1, 0, 0, R)
    for p in range(2):
        go(move_meta(p, 0, "+"))
        go(move_meta(p, 0, "-"))
        for h in range(2):
            go(move(h, p, 0, "+"))
            go(move(h, p, 0, "-"))
    for copy in share(0, 0):
        copy.wait_recv()
    go(ring_meta(1, 1))
    forward(1, 1, 0, R)
    pump(1, 0)
    line(-1)
    line(1)
    pump(1, 1)
    cross(0)
    for dx, dy in ((-1, 0), (1, 0), (0, -1), (0, 1)):
        give(dx, dy)
    pump(2, 0)
    for h in range(2):
        for sign in ("+", "-"):
            move(h, 0, 0, "f" + sign).wait_recv()
    move_meta(0, 0, "f+").wait_recv()
    go(move_meta(1, 2, "+"))
    go(move_meta(1, 2, "-"))
    for h in range(2):
        go(move(h, 1, 2, "+"))
        go(move(h, 1, 2, "-"))
    pump(2, 1)
    cross(-1)
    pump(3, 0)
    cross(1)
    cross_end(0)
    for dx, dy in ((-1, -1), (-1, 1), (1, -1), (1, 1), (2, 0), (0, 2)):
        give(dx, dy)
    pump(3, 1)
    pump(4, 0)
    cross(2)
    cross_end(-1)
    cross_end(1)
    for dx, dy in ((2, -1), (2, 1), (-1, 2), (1, 2)):
        give(dx, dy)
    pump(4, 1)
    cross_end(2)
    give(2, 2)
    pump(5, 0)
    pump(5, 1)
    acc_near[...] = jnp.full(acc_near.shape, -1.0, jnp.float32)
    acc_far[...] = jnp.full(acc_far.shape, -1.0, jnp.float32)

    def k_columns(first, n):
        for s in range(first, first + n):
            rows = pl.ds(s * R, R)
            kcl[rows, :] = column(km[s, 0:1, :])
            kgr[rows, :] = column(km[s, 1:2, :])

    def scores(sims, j, s_cl, s_gr, l_cl, l_gr):
        s = sims[:, j * R:(j + 1) * R]
        score = jnp.where(s_cl == l_cl, s, 0.5 * s)
        return jnp.where(s_gr == l_gr, score, -1.0)

    def block(s):
        if s == 0:
            return me, z
        d = (s + 1) // 2
        return (me if s % 2 else twin), (z - d * way) & 15

    before = sub > lax.broadcasted_iota(jnp.int32, (R, R), 1)

    def groups(q, first, n, near_side):
        out = []
        for s in range(first, first + n):
            nk, zk = block(s)
            if not near_side:
                ok = (q > nk) | ((q == nk) & (z > zk))
            elif s == 0:
                ok = (q < nk) | ((q == nk) & before)
            else:
                ok = (q < nk) | ((q == nk) & (zk > z))
            out.append(jnp.where(ok, kgr[s * R:(s + 1) * R, :], -1.0))
        return jnp.concatenate(out, axis=0) if n > 1 else out[0]

    def near(t, edge):
        stream = kb[0:NEAR_SLOTS].reshape(NEAR_SLOTS * R, D)
        lanes = qb[pl.ds(t * 4, 4)].reshape(TILE, D)
        sims = lax.dot_general(stream, lanes, NT, preferred_element_type=jnp.float32)
        rows = pl.ds(0, NEAR_SLOTS * R)
        best = acc_near[...]
        for j in range(4):
            q = t * 4 + j
            gr = groups(q, 0, NEAR_SLOTS, True) if edge else kgr[rows, :]
            best = jnp.maximum(best, scores(sims, j, kcl[rows, :], gr, qm[q, 0:1, :], qm[q, 1:2, :]))
        acc_near[...] = best

    def near_loop(lo, hi, edge=False):
        def body(t, carry):
            near(t, edge)
            return carry
        lax.fori_loop(lo, hi, body, 0)

    def far(t, first, n, edge):
        rows = pl.ds(first * R, n * R)
        stream = kb[first:first + n].reshape(n * R, D)
        lanes = qb[pl.ds(t * 8, 8)].reshape(2 * TILE, D)
        sims = lax.dot_general(stream, lanes, NT, preferred_element_type=jnp.float32)
        for j in range(8):
            q = t * 8 + j
            gr = groups(q, first, n, False) if edge else kgr[rows, :]
            best = scores(sims, j, kcl[rows, :], gr, qm[q, 0:1, :], qm[q, 1:2, :])
            where = pl.ds(pl.multiple_of(q * R, R), R)
            acc_far[:, where] = jnp.maximum(acc_far[:, where], jnp.max(best.reshape(n * R // 8, 8, R), axis=0))

    def far_loop(first, n):
        far(y, first, n, True)
        def body(t, carry):
            far(t, first, n, False)
            return carry
        lax.fori_loop(y + 1, NY, body, 0)

    k_columns(0, 11)
    for dy in range(NY):
        for dx in range(NX):
            if dx or dy:
                for copy in share(dx, dy):
                    copy.wait_recv()
    cut_a = y // 2
    cut_b = cut_a + (2 * y - cut_a + 1) // 2
    near_loop(2 * y, 2 * y + 2, True)
    near_loop(0, cut_a)
    far_loop(9, 2)
    pump(6, 0)
    pump(6, 1)
    k_columns(11, 2)
    near_loop(cut_a, cut_b)
    far_loop(11, 2)
    pump(7, 0)
    pump(7, 1)
    k_columns(13, 2)
    near_loop(cut_b, 2 * y)
    far_loop(13, 2)

    def back(s):
        d, o = (s + 1) // 2, (s + 1) % 2
        at = 2 * d - 1 + c
        return rc(near_out.at[s], near_in.at[at], ns.at[s], nr.at[at], dev(dz=-d * way, flip=o == 1))

    for s in range(NEAR_SLOTS):
        near_out[s] = jnp.max(acc_near[s * R:(s + 1) * R, :].T, axis=0, keepdims=True)
    for s in range(1, NEAR_SLOTS):
        go(back(s))
    pump(8, 0)
    k_columns(15, 1)
    far_loop(15, 1)

    for s in range(PLANE):
        far_out[s] = jnp.max(acc_far[:, s * R:(s + 1) * R], axis=0, keepdims=True)

    def reply(k):
        dx, dy, flip = k % NX, (k // NX) % NY, k >= NX * NY
        return rc(far_out.at[slot(dx, dy, flip)], far_in.at[k], fs.at[k], fr.at[k], dev(dx, dy, 0, flip))

    for k in range(1, PLANE):
        go(reply(k))
    best = jnp.maximum(near_out[0], far_out[me])
    for s in range(1, NEAR_SLOTS):
        rc(near_out.at[0], near_in.at[s], ns.at[0], nr.at[s], dev(dz=1)).wait_recv()
    for s in range(1, NEAR_SLOTS):
        best = jnp.maximum(best, near_in[s])
    for k in range(1, PLANE):
        reply(k).wait_recv()
    for k in range(1, PLANE):
        best = jnp.maximum(best, far_in[k])
    out_ref[...] = best
    for copy in pending:
        copy.wait_send()


def solution(mesh):
    def step(embeddings, cluster_id, cluster_group):
        dma = pltpu.SemaphoreType.DMA
        f32 = jnp.float32
        best = pl.pallas_call(
            kernel,
            out_shape=jax.ShapeDtypeStruct((1, R), f32),
            in_specs=[pl.BlockSpec(memory_space=pltpu.VMEM)] * 3,
            out_specs=pl.BlockSpec(memory_space=pltpu.VMEM),
            scratch_shapes=[
                pltpu.VMEM((NZ, R, D), jnp.bfloat16),
                pltpu.VMEM((PLANE, R, D), jnp.bfloat16),
                pltpu.VMEM((NZ, 2, R), f32),
                pltpu.VMEM((PLANE, 2, R), f32),
                pltpu.VMEM((NZ * R, R), f32),
                pltpu.VMEM((NZ * R, R), f32),
                pltpu.VMEM((NEAR_SLOTS * R, R), f32),
                pltpu.VMEM((8, PLANE * R), f32),
                pltpu.VMEM((NEAR_SLOTS, 1, R), f32),
                pltpu.VMEM((NEAR_SLOTS, 1, R), f32),
                pltpu.VMEM((PLANE, 1, R), f32),
                pltpu.VMEM((PLANE, 1, R), f32),
                dma((2 * sum(CHUNKS),)), dma((2 * sum(CHUNKS),)), dma((NZ,)), dma((NZ,)),
                dma((40,)), dma((40,)), dma((15,)), dma((15,)),
                dma((16,)), dma((16,)), dma((16,)), dma((16,)),
                dma((NEAR_SLOTS,)), dma((NEAR_SLOTS,)), dma((PLANE,)), dma((PLANE,)),
            ],
            compiler_params=pltpu.CompilerParams(
                collective_id=0, has_side_effects=True, vmem_limit_bytes=60 * 2**20),
        )(embeddings, cluster_id.reshape(1, R), cluster_group.reshape(1, -1))
        return best.reshape(R)

    placed = (P(("clu", "grp"), None), P(("clu", "grp")), P())
    return jax.shard_map(step, mesh=mesh, in_specs=placed, out_specs=P(("clu", "grp")), check_vma=False)
```

```python
import functools

import jax
import jax.numpy as jnp
from jax import lax
from jax.experimental import pallas as pl
from jax.experimental.pallas import tpu as pltpu
from jax.sharding import PartitionSpec as P

MESH = pl.DeviceIdType.MESH
NX, NY, NZ, NC = 4, 4, 16, 2
R, D = 128, 512
NEAR = 4
NEAR_SLOTS = 2 * NEAR + 1
FAR_SLOTS = NZ - NEAR_SLOTS
PLANE = NX * NY * NC
TILE = 4 * R
NT = (((1,), (1,)), ((), ()))
CHUNKS = (0, 4, 4, 4, 4, 4, 1, 1, 1)
START = tuple(2 * sum(CHUNKS[:d]) for d in range(NZ // 2 + 1))


def kernel(
    emb_hbm, cid_hbm, table_hbm, out_ref,
    emb_ref, cid_ref, table_ref, kb, qb, km, qm, kcl, kgr, acc_q, acc_k,
    k_out, k_in, q_out, q_in,
    ins, zs, zr, zms, zmr, qs, qr, qms, qmr, ds, dr, dms, dmr, ns, nr, fs, fr,
):
    clu, grp = lax.axis_index("clu"), lax.axis_index("grp")
    x, z = clu // NZ, clu % NZ
    y, c = grp // NC, grp % NC
    row = y * NC + c
    me = row * NX + x

    def dev(dx=0, dy=0, dz=0, flip=False):
        xx, yy, zz = (x + dx) & 3, (y + dy) & 3, (z + dz) & 15
        cc = 1 - c if flip else c
        return (xx * NZ + zz, yy * NC + cc)

    def slot(dx, dy, flip=False):
        cc = 1 - c if flip else c
        return (((y + dy) & 3) * NC + cc) * NX + ((x + dx) & 3)

    fetch = [pltpu.make_async_copy(a, b, ins.at[i]) for i, (a, b) in enumerate(
        ((emb_hbm, emb_ref), (cid_hbm, cid_ref), (table_hbm, table_ref)))]
    for copy in fetch:
        copy.start()
    barrier = pltpu.get_barrier_semaphore()
    for step in (dict(dx=1), dict(dx=-1), dict(dy=1), dict(dy=-1), dict(dz=1), dict(dz=-1), dict(flip=True)):
        pl.semaphore_signal(barrier, inc=1, device_id=dev(**step), device_id_type=MESH)

    fetch[0].wait()
    values = emb_ref[...].astype(jnp.float32)
    scale = lax.rsqrt(jnp.sum(values * values, axis=1, keepdims=True) + 1e-06)
    unit = (values * scale).astype(jnp.bfloat16)
    kb[0] = unit
    qb[me] = unit
    pending = []

    def rc(src, dst, s, r, where):
        return pltpu.make_async_remote_copy(
            src_ref=src, dst_ref=dst, send_sem=s, recv_sem=r, device_id=where, device_id_type=MESH)

    def go(copy):
        copy.start()
        pending.append(copy)

    half = R // 2
    way = 1 - 2 * c
    twin = slot(0, 0, True)

    def ring(d, o, part):
        n = R // CHUNKS[d]
        rows = pl.ds(part * n, n)
        if d == 1:
            src = kb.at[0, rows] if o == 0 else qb.at[twin, rows]
        else:
            src = kb.at[2 * d - 3 + o, rows]
        i = START[d] + o * CHUNKS[d] + part
        return rc(src, kb.at[2 * d - 1 + o, rows], zs.at[i], zr.at[i], dev(dz=way))

    def ring_meta(d, o):
        if d == 1:
            src = km.at[0] if o == 0 else qm.at[twin]
        else:
            src = km.at[2 * d - 3 + o]
        i = 2 * d - 1 + o
        return rc(src, km.at[i], zms.at[i], zmr.at[i], dev(dz=way))

    def forward(d, o, lo, hi):
        for part in range(CHUNKS[d]):
            if lo < (part + 1) * (R // CHUNKS[d]) <= hi:
                go(ring(d, o, part))

    def pump(d, o):
        ring_meta(d, o).wait_recv()
        more = d < 7 or (d == 7 and o == 0)
        if more:
            go(ring_meta(d + 1, o))
        n = R // CHUNKS[d]
        for part in range(CHUNKS[d]):
            ring(d, o, part).wait_recv()
            if more:
                forward(d + 1, o, part * n, (part + 1) * n)

    def move(h, phase, other, kind):
        along_x = (h == 0) == (phase == 0)
        step = 1 if kind[-1] == "+" else -1
        lo, n = h * half, half
        off = 0
        if kind[0] == "f":
            n = half // 2
            lo += 0 if step > 0 else n
            off = -step
        if along_x:
            s = slot(off, other if phase == 1 else 0)
            target = dev(dx=step)
        else:
            s = slot(other if phase == 1 else 0, off)
            target = dev(dy=step)
        i = h * 20 + (0 if phase == 0 else 4 + 4 * (other % 4)) + ("+", "-", "f+", "f-").index(kind)
        ref = qb.at[s, pl.ds(lo, n)]
        return rc(ref, ref, qs.at[i], qr.at[i], target)

    def move_meta(phase, other, kind):
        step = -1 if kind == "-" else 1
        off = -1 if kind == "f+" else 0
        if phase == 0:
            s, target = slot(off, 0), dev(dx=step)
        else:
            s, target = slot(other, off), dev(dy=step)
        i = (0 if phase == 0 else 3 + 3 * (other % 4)) + ("+", "-", "f+").index(kind)
        return rc(qm.at[s], qm.at[s], qms.at[i], qmr.at[i], target)

    def share(dx, dy):
        s = slot(dx, dy)
        i = (dy % 4) * 4 + dx % 4
        return (rc(qb.at[s], qb.at[s], ds.at[i], dr.at[i], dev(flip=True)),
                rc(qm.at[s], qm.at[s], dms.at[i], dmr.at[i], dev(flip=True)))

    def give(dx, dy):
        for copy in share(dx, dy):
            go(copy)


    def line(off):
        sign = "+" if off < 0 else "-"
        for h in range(2):
            move(h, 0, 0, sign).wait_recv()
            go(move(h, 0, 0, "f" + sign))
        move_meta(0, 0, sign).wait_recv()
        if sign == "+":
            go(move_meta(0, 0, "f+"))
        go(move_meta(1, off, "+"))
        go(move_meta(1, off, "-"))
        for h in range(2):
            go(move(h, 1, off, "+"))
            go(move(h, 1, off, "-"))

    def cross(off):
        for sign in ("+", "-"):
            for h in range(2):
                move(h, 1, off, sign).wait_recv()
                go(move(h, 1, off, "f" + sign))
            move_meta(1, off, sign).wait_recv()
        go(move_meta(1, off, "f+"))

    def cross_end(off):
        for h in range(2):
            for sign in ("+", "-"):
                move(h, 1, off, "f" + sign).wait_recv()
        move_meta(1, off, "f+").wait_recv()

    pl.semaphore_wait(barrier, 7)
    own_share = share(0, 0)
    go(own_share[0])
    forward(1, 0, 0, R)
    for p in range(2):
        for h in range(2):
            go(move(h, p, 0, "+"))
            go(move(h, p, 0, "-"))

    fetch[1].wait()
    fetch[2].wait()
    eye = lax.broadcasted_iota(jnp.int32, (R, R), 0) == lax.broadcasted_iota(jnp.int32, (R, R), 1)
    sub = lax.broadcasted_iota(jnp.int32, (R, R), 0)
    ones = jnp.ones((R, R), jnp.bfloat16)

    def column(line):
        spread = jnp.where(eye, jnp.broadcast_to(line, (R, R)), 0.0).astype(jnp.bfloat16)
        return jnp.dot(spread, ones, preferred_element_type=jnp.float32)

    cid = cid_ref[...]
    group = jnp.zeros((1, R), jnp.float32)
    for h in range(2):
        part = column(table_ref[:, h * R:(h + 1) * R].astype(jnp.float32))
        group += jnp.sum(jnp.where(jnp.broadcast_to(cid, (R, R)) == sub + h * R, part, 0.0), axis=0, keepdims=True)
    cluster = cid.astype(jnp.float32)
    km[0, 0:1, :] = cluster
    km[0, 1:2, :] = group
    qm[me, 0:1, :] = cluster
    qm[me, 1:2, :] = group

    go(own_share[1])
    go(ring_meta(1, 0))
    for p in range(2):
        go(move_meta(p, 0, "+"))
        go(move_meta(p, 0, "-"))
    own_share[0].wait_recv()
    forward(1, 1, 0, R)
    own_share[1].wait_recv()
    go(ring_meta(1, 1))
    pump(1, 0)
    pump(1, 1)
    line(-1)
    line(1)
    pump(2, 0)
    cross(0)
    for dx, dy in ((-1, 0), (1, 0), (0, -1), (0, 1)):
        give(dx, dy)
    pump(2, 1)
    for h in range(2):
        for sign in ("+", "-"):
            move(h, 0, 0, "f" + sign).wait_recv()
    move_meta(0, 0, "f+").wait_recv()
    go(move_meta(1, 2, "+"))
    go(move_meta(1, 2, "-"))
    for h in range(2):
        go(move(h, 1, 2, "+"))
        go(move(h, 1, 2, "-"))
    cross(-1)
    pump(3, 0)
    cross(1)
    cross_end(0)
    for dx, dy in ((-1, -1), (-1, 1), (1, -1), (1, 1), (2, 0), (0, 2)):
        give(dx, dy)
    pump(3, 1)
    pump(4, 0)
    cross(2)
    cross_end(-1)
    cross_end(1)
    for dx, dy in ((2, -1), (2, 1), (-1, 2), (1, 2)):
        give(dx, dy)
    pump(4, 1)
    acc_q[...] = jnp.full(acc_q.shape, -1.0, jnp.float32)
    acc_k[...] = jnp.full(acc_k.shape, -1.0, jnp.float32)

    def k_columns(first, n):
        for s in range(first, first + n):
            rows = pl.ds(s * R, R)
            kcl[rows, :] = column(km[s, 0:1, :])
            kgr[rows, :] = column(km[s, 1:2, :])

    def scores(sims, j, s_cl, s_gr, l_cl, l_gr):
        s = sims[:, j * R:(j + 1) * R]
        score = jnp.where(s_cl == l_cl, s, 0.5 * s)
        return jnp.where(s_gr == l_gr, score, -1.0)

    def block(s):
        if s == 0:
            return me, z
        d = (s + 1) // 2
        return (me if s % 2 else twin), (z - d * way) & 15

    before = sub < lax.broadcasted_iota(jnp.int32, (R, R), 1)

    def groups(q, first, n, near_side):
        out = []
        for s in range(first, first + n):
            nk, zk = block(s)
            if not near_side:
                ok = (q < nk) | ((q == nk) & (zk > z))
            elif s == 0:
                ok = (q > nk) | ((q == nk) & before)
            else:
                ok = (q > nk) | ((q == nk) & (z > zk))
            out.append(jnp.where(ok, kgr[s * R:(s + 1) * R, :], -1.0))
        return jnp.concatenate(out, axis=0) if n > 1 else out[0]

    def near(t, edge):
        stream = kb[0:NEAR_SLOTS].reshape(NEAR_SLOTS * R, D)
        lanes = qb[pl.ds(t * 4, 4)].reshape(TILE, D)
        sims = lax.dot_general(stream, lanes, NT, preferred_element_type=jnp.float32)
        rows = pl.ds(0, NEAR_SLOTS * R)
        for j in range(4):
            q = t * 4 + j
            gr = groups(q, 0, NEAR_SLOTS, True) if edge else kgr[rows, :]
            best = scores(sims, j, kcl[rows, :], gr, qm[q, 0:1, :], qm[q, 1:2, :])
            where = pl.ds(pl.multiple_of(q * R, R), R)
            acc_q[:, where] = jnp.max(best.reshape(NEAR_SLOTS * R // 8, 8, R), axis=0)

    def near_loop(lo, hi, edge=False):
        def body(t, carry):
            near(t, edge)
            return carry
        lax.fori_loop(lo, hi, body, 0)

    def far(t, first, n, edge):
        rows = pl.ds(first * R, n * R)
        stream = kb[first:first + n].reshape(n * R, D)
        lanes = qb[pl.ds(t * 8, 8)].reshape(2 * TILE, D)
        sims = lax.dot_general(stream, lanes, NT, preferred_element_type=jnp.float32)
        at = pl.ds((first - NEAR_SLOTS) * R, n * R)
        best = acc_k[at, :]
        for j in range(8):
            q = t * 8 + j
            gr = groups(q, first, n, False) if edge else kgr[rows, :]
            best = jnp.maximum(best, scores(sims, j, kcl[rows, :], gr, qm[q, 0:1, :], qm[q, 1:2, :]))
        acc_k[at, :] = best

    def far_loop(first, n):
        def body(t, carry):
            far(t, first, n, False)
            return carry
        lax.fori_loop(0, y, body, 0)
        far(y, first, n, True)

    def back(s):
        d, o = (s + 1) // 2, (s + 1) % 2
        at = 2 * (d - NEAR - 1) + (c if d < 8 else 0)
        i = s - NEAR_SLOTS
        return rc(k_out.at[i], k_in.at[at], ns.at[i], nr.at[at], dev(dz=-d * way, flip=o == 1))

    def send_back(first, n):
        for s in range(first, first + n):
            i = s - NEAR_SLOTS
            k_out[i] = jnp.max(acc_k[i * R:(i + 1) * R, :].T, axis=0, keepdims=True)
            go(back(s))

    def reply(k):
        dx, dy, flip = k % NX, (k // NX) % NY, k >= NX * NY
        return rc(q_out.at[slot(dx, dy, flip)], q_in.at[k], fs.at[k], fr.at[k], dev(dx, dy, 0, flip))

    k_columns(0, NEAR_SLOTS)
    for dx in range(1, NX):
        for copy in share(dx, 0):
            copy.wait_recv()
    near_loop(2 * y, 2 * y + 2, True)
    cross_end(2)
    give(2, 2)
    pump(5, 0)
    pump(5, 1)
    k_columns(9, 2)
    for dy in range(1, NY):
        for dx in range(NX):
            for copy in share(dx, dy):
                copy.wait_recv()
    cut = 2 * y + 2 + (6 - 2 * y) // 2
    near_loop(2 * y + 2, cut)
    far_loop(9, 2)
    pump(6, 0)
    pump(6, 1)
    k_columns(11, 2)
    near_loop(cut, PLANE // 4)
    for s in range(PLANE):
        q_out[s] = jnp.max(acc_q[:, s * R:(s + 1) * R], axis=0, keepdims=True)
    pump(7, 0)
    pump(7, 1)
    for k in range(1, PLANE):
        go(reply(k))
    far_loop(11, 2)
    k_columns(13, 2)
    far_loop(13, 2)
    send_back(9, 6)
    best = q_out[me]
    for k in range(1, PLANE):
        reply(k).wait_recv()
    for k in range(1, PLANE):
        best = jnp.maximum(best, q_in[k])
    pump(8, 0)
    k_columns(15, 1)
    far_loop(15, 1)
    send_back(15, 1)
    for s in range(FAR_SLOTS):
        rc(k_out.at[0], k_in.at[s], ns.at[0], nr.at[s], dev(dz=1)).wait_recv()
    for s in range(FAR_SLOTS):
        best = jnp.maximum(best, k_in[s])
    out_ref[...] = best
    for copy in pending:
        copy.wait_send()


def solution(mesh):
    def step(embeddings, cluster_id, cluster_group):
        dma = pltpu.SemaphoreType.DMA
        f32 = jnp.float32
        best = pl.pallas_call(
            kernel,
            out_shape=jax.ShapeDtypeStruct((1, R), f32),
            in_specs=[pl.BlockSpec(memory_space=pl.ANY)] * 3,
            out_specs=pl.BlockSpec(memory_space=pltpu.VMEM),
            scratch_shapes=[
                pltpu.VMEM((R, D), jnp.bfloat16),
                pltpu.VMEM((1, R), jnp.int32),
                pltpu.VMEM((1, cluster_group.shape[0]), jnp.int32),
                pltpu.VMEM((NZ, R, D), jnp.bfloat16),
                pltpu.VMEM((PLANE, R, D), jnp.bfloat16),
                pltpu.VMEM((NZ, 2, R), f32),
                pltpu.VMEM((PLANE, 2, R), f32),
                pltpu.VMEM((NZ * R, R), f32),
                pltpu.VMEM((NZ * R, R), f32),
                pltpu.VMEM((8, PLANE * R), f32),
                pltpu.VMEM((FAR_SLOTS * R, R), f32),
                pltpu.VMEM((FAR_SLOTS, 1, R), f32),
                pltpu.VMEM((FAR_SLOTS, 1, R), f32),
                pltpu.VMEM((PLANE, 1, R), f32),
                pltpu.VMEM((PLANE, 1, R), f32),
                dma((3,)),
                dma((2 * sum(CHUNKS),)), dma((2 * sum(CHUNKS),)), dma((NZ,)), dma((NZ,)),
                dma((40,)), dma((40,)), dma((15,)), dma((15,)),
                dma((16,)), dma((16,)), dma((16,)), dma((16,)),
                dma((FAR_SLOTS,)), dma((FAR_SLOTS,)), dma((PLANE,)), dma((PLANE,)),
            ],
            compiler_params=pltpu.CompilerParams(
                collective_id=0, has_side_effects=True, vmem_limit_bytes=60 * 2**20),
        )(embeddings, cluster_id.reshape(1, R), cluster_group.reshape(1, -1))
        return best.reshape(R)

    placed = (P(("clu", "grp"), None), P(("clu", "grp")), P())
    return jax.shard_map(step, mesh=mesh, in_specs=placed, out_specs=P(("clu", "grp")), check_vma=False)
```

```python
import functools

import jax
import jax.numpy as jnp
from jax import lax
from jax.experimental import pallas as pl
from jax.experimental.pallas import tpu as pltpu
from jax.sharding import PartitionSpec as P

MESH = pl.DeviceIdType.MESH
NX, NY, NZ, NC = 4, 4, 16, 2
R, D = 128, 512
NEAR = 4
NEAR_SLOTS = 2 * NEAR + 1
PLANE = NX * NY * NC
TILE = 4 * R
NT = (((1,), (1,)), ((), ()))
CHUNKS = (0, 4, 4, 4, 4, 4, 1, 1, 1)
START = tuple(2 * sum(CHUNKS[:d]) for d in range(NZ // 2 + 1))


def kernel(
    emb_hbm, cid_hbm, table_hbm, out_ref,
    emb_ref, cid_ref, table_ref, kb, qb, km, qm, kcl, kgr, acc_q, acc_k,
    k_out, k_in, q_out, q_in,
    ins, zs, zr, zms, zmr, qs, qr, qms, qmr, ds, dr, dms, dmr, ns, nr, fs, fr,
):
    clu, grp = lax.axis_index("clu"), lax.axis_index("grp")
    x, z = clu // NZ, clu % NZ
    y, c = grp // NC, grp % NC
    row = y * NC + c
    me = row * NX + x

    def dev(dx=0, dy=0, dz=0, flip=False):
        xx, yy, zz = (x + dx) & 3, (y + dy) & 3, (z + dz) & 15
        cc = 1 - c if flip else c
        return (xx * NZ + zz, yy * NC + cc)

    def slot(dx, dy, flip=False):
        cc = 1 - c if flip else c
        return (((y + dy) & 3) * NC + cc) * NX + ((x + dx) & 3)

    fetch = [pltpu.make_async_copy(a, b, ins.at[i]) for i, (a, b) in enumerate(
        ((emb_hbm, emb_ref), (cid_hbm, cid_ref), (table_hbm, table_ref)))]
    for copy in fetch:
        copy.start()
    barrier = pltpu.get_barrier_semaphore()
    for step in (dict(dx=1), dict(dx=-1), dict(dy=1), dict(dy=-1), dict(dz=1), dict(dz=-1), dict(flip=True)):
        pl.semaphore_signal(barrier, inc=1, device_id=dev(**step), device_id_type=MESH)

    fetch[0].wait()
    values = emb_ref[...].astype(jnp.float32)
    scale = lax.rsqrt(jnp.sum(values * values, axis=1, keepdims=True) + 1e-06)
    unit = (values * scale).astype(jnp.bfloat16)
    kb[0] = unit
    qb[me] = unit
    pending = []

    def rc(src, dst, s, r, where):
        return pltpu.make_async_remote_copy(
            src_ref=src, dst_ref=dst, send_sem=s, recv_sem=r, device_id=where, device_id_type=MESH)

    def go(copy):
        copy.start()
        pending.append(copy)

    half = R // 2
    way = 1 - 2 * c
    twin = slot(0, 0, True)

    def ring(d, o, part):
        n = R // CHUNKS[d]
        rows = pl.ds(part * n, n)
        if d == 1:
            src = kb.at[0, rows] if o == 0 else qb.at[twin, rows]
        else:
            src = kb.at[2 * d - 3 + o, rows]
        i = START[d] + o * CHUNKS[d] + part
        return rc(src, kb.at[2 * d - 1 + o, rows], zs.at[i], zr.at[i], dev(dz=way))

    def ring_meta(d, o):
        if d == 1:
            src = km.at[0] if o == 0 else qm.at[twin]
        else:
            src = km.at[2 * d - 3 + o]
        i = 2 * d - 1 + o
        return rc(src, km.at[i], zms.at[i], zmr.at[i], dev(dz=way))

    def forward(d, o, lo, hi):
        for part in range(CHUNKS[d]):
            if lo < (part + 1) * (R // CHUNKS[d]) <= hi:
                go(ring(d, o, part))

    def pump(d, o):
        ring_meta(d, o).wait_recv()
        more = d < 7 or (d == 7 and o == 0)
        if more:
            go(ring_meta(d + 1, o))
        n = R // CHUNKS[d]
        for part in range(CHUNKS[d]):
            ring(d, o, part).wait_recv()
            if more:
                forward(d + 1, o, part * n, (part + 1) * n)

    def move(h, phase, other, kind):
        along_x = (h == 0) == (phase == 0)
        step = 1 if kind[-1] == "+" else -1
        lo, n = h * half, half
        off = 0
        if kind[0] == "f":
            n = half // 2
            lo += 0 if step > 0 else n
            off = -step
        if along_x:
            s = slot(off, other if phase == 1 else 0)
            target = dev(dx=step)
        else:
            s = slot(other if phase == 1 else 0, off)
            target = dev(dy=step)
        i = h * 20 + (0 if phase == 0 else 4 + 4 * (other % 4)) + ("+", "-", "f+", "f-").index(kind)
        ref = qb.at[s, pl.ds(lo, n)]
        return rc(ref, ref, qs.at[i], qr.at[i], target)

    def move_meta(phase, other, kind):
        step = -1 if kind == "-" else 1
        off = -1 if kind == "f+" else 0
        if phase == 0:
            s, target = slot(off, 0), dev(dx=step)
        else:
            s, target = slot(other, off), dev(dy=step)
        i = (0 if phase == 0 else 3 + 3 * (other % 4)) + ("+", "-", "f+").index(kind)
        return rc(qm.at[s], qm.at[s], qms.at[i], qmr.at[i], target)

    def share(dx, dy):
        s = slot(dx, dy)
        i = (dy % 4) * 4 + dx % 4
        return (rc(qb.at[s], qb.at[s], ds.at[i], dr.at[i], dev(flip=True)),
                rc(qm.at[s], qm.at[s], dms.at[i], dmr.at[i], dev(flip=True)))

    def give(dx, dy):
        for copy in share(dx, dy):
            go(copy)


    def line(off):
        sign = "+" if off < 0 else "-"
        for h in range(2):
            move(h, 0, 0, sign).wait_recv()
            go(move(h, 0, 0, "f" + sign))
        move_meta(0, 0, sign).wait_recv()
        if sign == "+":
            go(move_meta(0, 0, "f+"))
        go(move_meta(1, off, "+"))
        go(move_meta(1, off, "-"))
        for h in range(2):
            go(move(h, 1, off, "+"))
            go(move(h, 1, off, "-"))

    def cross(off):
        for sign in ("+", "-"):
            for h in range(2):
                move(h, 1, off, sign).wait_recv()
                go(move(h, 1, off, "f" + sign))
            move_meta(1, off, sign).wait_recv()
        go(move_meta(1, off, "f+"))

    def cross_end(off):
        for h in range(2):
            for sign in ("+", "-"):
                move(h, 1, off, "f" + sign).wait_recv()
        move_meta(1, off, "f+").wait_recv()

    pl.semaphore_wait(barrier, 7)
    own_share = share(0, 0)
    go(own_share[0])
    forward(1, 0, 0, R)
    for p in range(2):
        for h in range(2):
            go(move(h, p, 0, "+"))
            go(move(h, p, 0, "-"))

    fetch[1].wait()
    fetch[2].wait()
    eye = lax.broadcasted_iota(jnp.int32, (R, R), 0) == lax.broadcasted_iota(jnp.int32, (R, R), 1)
    sub = lax.broadcasted_iota(jnp.int32, (R, R), 0)
    ones = jnp.ones((R, R), jnp.bfloat16)

    def column(line):
        spread = jnp.where(eye, jnp.broadcast_to(line, (R, R)), 0.0).astype(jnp.bfloat16)
        return jnp.dot(spread, ones, preferred_element_type=jnp.float32)

    cid = cid_ref[...]
    group = jnp.zeros((1, R), jnp.float32)
    for h in range(2):
        part = column(table_ref[:, h * R:(h + 1) * R].astype(jnp.float32))
        group += jnp.sum(jnp.where(jnp.broadcast_to(cid, (R, R)) == sub + h * R, part, 0.0), axis=0, keepdims=True)
    cluster = cid.astype(jnp.float32)
    km[0, 0:1, :] = cluster
    km[0, 1:2, :] = group
    qm[me, 0:1, :] = cluster
    qm[me, 1:2, :] = group

    go(own_share[1])
    go(ring_meta(1, 0))
    for p in range(2):
        go(move_meta(p, 0, "+"))
        go(move_meta(p, 0, "-"))
    own_share[0].wait_recv()
    forward(1, 1, 0, R)
    own_share[1].wait_recv()
    go(ring_meta(1, 1))
    pump(1, 0)
    pump(1, 1)
    line(-1)
    line(1)
    pump(2, 0)
    cross(0)
    for dx, dy in ((-1, 0), (1, 0), (0, -1), (0, 1)):
        give(dx, dy)
    pump(2, 1)
    for h in range(2):
        for sign in ("+", "-"):
            move(h, 0, 0, "f" + sign).wait_recv()
    move_meta(0, 0, "f+").wait_recv()
    go(move_meta(1, 2, "+"))
    go(move_meta(1, 2, "-"))
    for h in range(2):
        go(move(h, 1, 2, "+"))
        go(move(h, 1, 2, "-"))
    cross(-1)
    pump(3, 0)
    cross(1)
    cross_end(0)
    for dx, dy in ((-1, -1), (-1, 1), (1, -1), (1, 1), (2, 0), (0, 2)):
        give(dx, dy)
    pump(3, 1)
    pump(4, 0)
    cross(2)
    cross_end(-1)
    cross_end(1)
    for dx, dy in ((2, -1), (2, 1), (-1, 2), (1, 2)):
        give(dx, dy)
    pump(4, 1)
    acc_q[...] = jnp.full(acc_q.shape, -1.0, jnp.float32)
    acc_k[...] = jnp.full(acc_k.shape, -1.0, jnp.float32)

    def k_columns(first, n):
        for s in range(first, first + n):
            rows = pl.ds(s * R, R)
            kcl[rows, :] = column(km[s, 0:1, :])
            kgr[rows, :] = column(km[s, 1:2, :])

    def scores(sims, j, s_cl, s_gr, l_cl, l_gr):
        s = sims[:, j * R:(j + 1) * R]
        score = jnp.where(s_cl == l_cl, s, 0.5 * s)
        return jnp.where(s_gr == l_gr, score, -1.0)

    def block(s):
        if s == 0:
            return me, z
        d = (s + 1) // 2
        return (me if s % 2 else twin), (z - d * way) & 15

    before = sub > lax.broadcasted_iota(jnp.int32, (R, R), 1)

    def groups(q, first, n, near_side):
        out = []
        for s in range(first, first + n):
            nk, zk = block(s)
            if not near_side:
                ok = (q > nk) | ((q == nk) & (z > zk))
            elif s == 0:
                ok = (q < nk) | ((q == nk) & before)
            else:
                ok = (q < nk) | ((q == nk) & (zk > z))
            out.append(jnp.where(ok, kgr[s * R:(s + 1) * R, :], -1.0))
        return jnp.concatenate(out, axis=0) if n > 1 else out[0]

    def near(t, edge):
        stream = kb[0:NEAR_SLOTS].reshape(NEAR_SLOTS * R, D)
        lanes = qb[pl.ds(t * 8, 8)].reshape(2 * TILE, D)
        sims = lax.dot_general(stream, lanes, NT, preferred_element_type=jnp.float32)
        rows = pl.ds(0, NEAR_SLOTS * R)
        best = acc_k[...]
        for j in range(8):
            q = t * 8 + j
            gr = groups(q, 0, NEAR_SLOTS, True) if edge else kgr[rows, :]
            best = jnp.maximum(best, scores(sims, j, kcl[rows, :], gr, qm[q, 0:1, :], qm[q, 1:2, :]))
        acc_k[...] = best

    def near_loop(lo, hi):
        def body(t, carry):
            near(t, False)
            return carry
        lax.fori_loop(lo, hi, body, 0)

    def far(t, first, n, edge):
        rows = pl.ds(first * R, n * R)
        stream = kb[first:first + n].reshape(n * R, D)
        lanes = qb[pl.ds(t * 8, 8)].reshape(2 * TILE, D)
        sims = lax.dot_general(stream, lanes, NT, preferred_element_type=jnp.float32)
        for j in range(8):
            q = t * 8 + j
            gr = groups(q, first, n, False) if edge else kgr[rows, :]
            best = scores(sims, j, kcl[rows, :], gr, qm[q, 0:1, :], qm[q, 1:2, :])
            where = pl.ds(pl.multiple_of(q * R, R), R)
            acc_q[:, where] = jnp.maximum(acc_q[:, where], jnp.max(best.reshape(n * R // 8, 8, R), axis=0))

    def far_loop(first, n):
        def body(t, carry):
            far(t, first, n, False)
            return carry
        lax.fori_loop(y + 1, NY, body, 0)
        far(y, first, n, True)

    def back(s):
        d, o = (s + 1) // 2, (s + 1) % 2
        at = 2 * d - 1 + c
        return rc(k_out.at[s], k_in.at[at], ns.at[s], nr.at[at], dev(dz=-d * way, flip=o == 1))

    def reply(k):
        dx, dy, flip = k % NX, (k // NX) % NY, k >= NX * NY
        return rc(q_out.at[slot(dx, dy, flip)], q_in.at[k], fs.at[k], fr.at[k], dev(dx, dy, 0, flip))

    def hops(k):
        dx, dy = k % NX, (k // NX) % NY
        return min(dx, NX - dx) + min(dy, NY - dy)

    def plane_result(k):
        dx, dy, flip = k % NX, (k // NX) % NY, k >= NX * NY
        s = slot(dx, dy, flip)
        return s, jnp.max(acc_q[:, pl.ds(pl.multiple_of(s * R, R), R)], axis=0, keepdims=True)

    k_columns(0, NEAR_SLOTS)
    for dx in range(1, NX):
        for copy in share(dx, 0):
            copy.wait_recv()
    near(y, True)
    cross_end(2)
    give(2, 2)
    pump(5, 0)
    pump(5, 1)
    k_columns(9, 2)
    for dy in range(1, NY):
        for dx in range(NX):
            for copy in share(dx, dy):
                copy.wait_recv()
    cut_a = (y + 2) // 3
    cut_b = cut_a + (y - cut_a + 1) // 2
    near_loop(0, cut_a)
    far_loop(9, 2)
    pump(6, 0)
    pump(6, 1)
    k_columns(11, 2)
    near_loop(cut_a, cut_b)
    far_loop(11, 2)
    pump(7, 0)
    pump(7, 1)
    near_loop(cut_b, y)
    for s in range(NEAR_SLOTS):
        k_out[s] = jnp.max(acc_k[s * R:(s + 1) * R, :].T, axis=0, keepdims=True)
    for s in range(1, NEAR_SLOTS):
        go(back(s))
    k_columns(13, 2)
    far_loop(13, 2)
    pump(8, 0)
    k_columns(15, 1)
    far_loop(15, 1)
    for k in sorted(range(1, PLANE), key=hops, reverse=True):
        s, result = plane_result(k)
        q_out[s] = result
        go(reply(k))
    best = jnp.maximum(k_out[0], plane_result(0)[1])
    for s in range(1, NEAR_SLOTS):
        rc(k_out.at[0], k_in.at[s], ns.at[0], nr.at[s], dev(dz=1)).wait_recv()
    for s in range(1, NEAR_SLOTS):
        best = jnp.maximum(best, k_in[s])
    for k in range(1, PLANE):
        reply(k).wait_recv()
    for k in range(1, PLANE):
        best = jnp.maximum(best, q_in[k])
    out_ref[...] = best
    for copy in pending:
        copy.wait_send()


def solution(mesh):
    def step(embeddings, cluster_id, cluster_group):
        dma = pltpu.SemaphoreType.DMA
        f32 = jnp.float32
        best = pl.pallas_call(
            kernel,
            out_shape=jax.ShapeDtypeStruct((1, R), f32),
            in_specs=[pl.BlockSpec(memory_space=pl.ANY)] * 3,
            out_specs=pl.BlockSpec(memory_space=pltpu.VMEM),
            scratch_shapes=[
                pltpu.VMEM((R, D), jnp.bfloat16),
                pltpu.VMEM((1, R), jnp.int32),
                pltpu.VMEM((1, cluster_group.shape[0]), jnp.int32),
                pltpu.VMEM((NZ, R, D), jnp.bfloat16),
                pltpu.VMEM((PLANE, R, D), jnp.bfloat16),
                pltpu.VMEM((NZ, 2, R), f32),
                pltpu.VMEM((PLANE, 2, R), f32),
                pltpu.VMEM((NZ * R, R), f32),
                pltpu.VMEM((NZ * R, R), f32),
                pltpu.VMEM((8, PLANE * R), f32),
                pltpu.VMEM((NEAR_SLOTS * R, R), f32),
                pltpu.VMEM((NEAR_SLOTS, 1, R), f32),
                pltpu.VMEM((NEAR_SLOTS, 1, R), f32),
                pltpu.VMEM((PLANE, 1, R), f32),
                pltpu.VMEM((PLANE, 1, R), f32),
                dma((3,)),
                dma((2 * sum(CHUNKS),)), dma((2 * sum(CHUNKS),)), dma((NZ,)), dma((NZ,)),
                dma((40,)), dma((40,)), dma((15,)), dma((15,)),
                dma((16,)), dma((16,)), dma((16,)), dma((16,)),
                dma((NEAR_SLOTS,)), dma((NEAR_SLOTS,)), dma((PLANE,)), dma((PLANE,)),
            ],
            compiler_params=pltpu.CompilerParams(
                collective_id=0, has_side_effects=True, vmem_limit_bytes=60 * 2**20),
        )(embeddings, cluster_id.reshape(1, R), cluster_group.reshape(1, -1))
        return best.reshape(R)

    placed = (P(("clu", "grp"), None), P(("clu", "grp")), P())
    return jax.shard_map(step, mesh=mesh, in_specs=placed, out_specs=P(("clu", "grp")), check_vma=False)
```

```python
import functools

import jax
import jax.numpy as jnp
from jax import lax
from jax.experimental import pallas as pl
from jax.experimental.pallas import tpu as pltpu
from jax.sharding import PartitionSpec as P

MESH = pl.DeviceIdType.MESH
NX, NY, NZ, NC = 4, 4, 16, 2
R, D = 128, 512
NEAR = 4
NEAR_SLOTS = 2 * NEAR + 1
PLANE = NX * NY * NC
TILE = 4 * R
NT = (((1,), (1,)), ((), ()))
CHUNKS = (0, 4, 4, 4, 4, 4, 1, 1, 1)
START = tuple(2 * sum(CHUNKS[:d]) for d in range(NZ // 2 + 1))


def kernel(
    emb_hbm, cid_hbm, table_hbm, out_ref,
    emb_ref, cid_ref, table_ref, kb, qb, km, qm, kcl, kgr, acc_q, acc_k,
    k_out, k_in, q_out, q_in,
    ins, zs, zr, zms, zmr, qs, qr, qms, qmr, ds, dr, dms, dmr, ns, nr, fs, fr,
):
    clu, grp = lax.axis_index("clu"), lax.axis_index("grp")
    x, z = clu // NZ, clu % NZ
    y, c = grp // NC, grp % NC
    row = y * NC + c
    me = row * NX + x

    def dev(dx=0, dy=0, dz=0, flip=False):
        xx, yy, zz = (x + dx) & 3, (y + dy) & 3, (z + dz) & 15
        cc = 1 - c if flip else c
        return (xx * NZ + zz, yy * NC + cc)

    def slot(dx, dy, flip=False):
        cc = 1 - c if flip else c
        return (((y + dy) & 3) * NC + cc) * NX + ((x + dx) & 3)

    fetch = [pltpu.make_async_copy(a, b, ins.at[i]) for i, (a, b) in enumerate(
        ((emb_hbm, emb_ref), (cid_hbm, cid_ref), (table_hbm, table_ref)))]
    for copy in fetch:
        copy.start()
    barrier = pltpu.get_barrier_semaphore()
    for step in (dict(dx=1), dict(dx=-1), dict(dy=1), dict(dy=-1), dict(dz=1), dict(dz=-1), dict(flip=True)):
        pl.semaphore_signal(barrier, inc=1, device_id=dev(**step), device_id_type=MESH)

    fetch[0].wait()
    values = emb_ref[...].astype(jnp.float32)
    scale = lax.rsqrt(jnp.sum(values * values, axis=1, keepdims=True) + 1e-06)
    unit = (values * scale).astype(jnp.bfloat16)
    kb[0] = unit
    qb[me] = unit
    pending = []

    def rc(src, dst, s, r, where):
        return pltpu.make_async_remote_copy(
            src_ref=src, dst_ref=dst, send_sem=s, recv_sem=r, device_id=where, device_id_type=MESH)

    def go(copy):
        copy.start()
        pending.append(copy)

    half = R // 2
    way = 1 - 2 * c
    twin = slot(0, 0, True)

    def ring(d, o, part):
        n = R // CHUNKS[d]
        rows = pl.ds(part * n, n)
        if d == 1:
            src = kb.at[0, rows] if o == 0 else qb.at[twin, rows]
        else:
            src = kb.at[2 * d - 3 + o, rows]
        i = START[d] + o * CHUNKS[d] + part
        return rc(src, kb.at[2 * d - 1 + o, rows], zs.at[i], zr.at[i], dev(dz=way))

    def ring_meta(d, o):
        if d == 1:
            src = km.at[0] if o == 0 else qm.at[twin]
        else:
            src = km.at[2 * d - 3 + o]
        i = 2 * d - 1 + o
        return rc(src, km.at[i], zms.at[i], zmr.at[i], dev(dz=way))

    def forward(d, o, lo, hi):
        for part in range(CHUNKS[d]):
            if lo < (part + 1) * (R // CHUNKS[d]) <= hi:
                go(ring(d, o, part))

    def pump(d, o):
        ring_meta(d, o).wait_recv()
        more = d < 7 or (d == 7 and o == 0)
        if more:
            go(ring_meta(d + 1, o))
        n = R // CHUNKS[d]
        for part in range(CHUNKS[d]):
            ring(d, o, part).wait_recv()
            if more:
                forward(d + 1, o, part * n, (part + 1) * n)

    def move(h, phase, other, kind):
        along_x = (h == 0) == (phase == 0)
        step = 1 if kind[-1] == "+" else -1
        lo, n = h * half, half
        off = 0
        if kind[0] == "f":
            n = half // 2
            lo += 0 if step > 0 else n
            off = -step
        if along_x:
            s = slot(off, other if phase == 1 else 0)
            target = dev(dx=step)
        else:
            s = slot(other if phase == 1 else 0, off)
            target = dev(dy=step)
        i = h * 20 + (0 if phase == 0 else 4 + 4 * (other % 4)) + ("+", "-", "f+", "f-").index(kind)
        ref = qb.at[s, pl.ds(lo, n)]
        return rc(ref, ref, qs.at[i], qr.at[i], target)

    def move_meta(phase, other, kind):
        step = -1 if kind == "-" else 1
        off = -1 if kind == "f+" else 0
        if phase == 0:
            s, target = slot(off, 0), dev(dx=step)
        else:
            s, target = slot(other, off), dev(dy=step)
        i = (0 if phase == 0 else 3 + 3 * (other % 4)) + ("+", "-", "f+").index(kind)
        return rc(qm.at[s], qm.at[s], qms.at[i], qmr.at[i], target)

    def share(dx, dy):
        s = slot(dx, dy)
        i = (dy % 4) * 4 + dx % 4
        return (rc(qb.at[s], qb.at[s], ds.at[i], dr.at[i], dev(flip=True)),
                rc(qm.at[s], qm.at[s], dms.at[i], dmr.at[i], dev(flip=True)))

    def give(dx, dy):
        for copy in share(dx, dy):
            go(copy)


    def line(off):
        sign = "+" if off < 0 else "-"
        for h in range(2):
            move(h, 0, 0, sign).wait_recv()
            go(move(h, 0, 0, "f" + sign))
        move_meta(0, 0, sign).wait_recv()
        if sign == "+":
            go(move_meta(0, 0, "f+"))
        go(move_meta(1, off, "+"))
        go(move_meta(1, off, "-"))
        for h in range(2):
            go(move(h, 1, off, "+"))
            go(move(h, 1, off, "-"))

    def cross(off):
        for sign in ("+", "-"):
            for h in range(2):
                move(h, 1, off, sign).wait_recv()
                go(move(h, 1, off, "f" + sign))
            move_meta(1, off, sign).wait_recv()
        go(move_meta(1, off, "f+"))

    def cross_end(off):
        for h in range(2):
            for sign in ("+", "-"):
                move(h, 1, off, "f" + sign).wait_recv()
        move_meta(1, off, "f+").wait_recv()

    pl.semaphore_wait(barrier, 7)
    own_share = share(0, 0)
    go(own_share[0])
    forward(1, 0, 0, R)
    for p in range(2):
        for h in range(2):
            go(move(h, p, 0, "+"))
            go(move(h, p, 0, "-"))

    fetch[1].wait()
    fetch[2].wait()
    eye = lax.broadcasted_iota(jnp.int32, (R, R), 0) == lax.broadcasted_iota(jnp.int32, (R, R), 1)
    sub = lax.broadcasted_iota(jnp.int32, (R, R), 0)
    ones = jnp.ones((R, R), jnp.bfloat16)

    def column(line):
        spread = jnp.where(eye, jnp.broadcast_to(line, (R, R)), 0.0).astype(jnp.bfloat16)
        return jnp.dot(spread, ones, preferred_element_type=jnp.float32)

    cid = cid_ref[...]
    group = jnp.zeros((1, R), jnp.float32)
    for h in range(2):
        part = column(table_ref[:, h * R:(h + 1) * R].astype(jnp.float32))
        group += jnp.sum(jnp.where(jnp.broadcast_to(cid, (R, R)) == sub + h * R, part, 0.0), axis=0, keepdims=True)
    cluster = cid.astype(jnp.float32)
    km[0, 0:1, :] = cluster
    km[0, 1:2, :] = group
    qm[me, 0:1, :] = cluster
    qm[me, 1:2, :] = group

    go(own_share[1])
    go(ring_meta(1, 0))
    for p in range(2):
        go(move_meta(p, 0, "+"))
        go(move_meta(p, 0, "-"))
    own_share[0].wait_recv()
    forward(1, 1, 0, R)
    own_share[1].wait_recv()
    go(ring_meta(1, 1))
    pump(1, 0)
    line(-1)
    line(1)
    pump(1, 1)
    cross(0)
    for dx, dy in ((-1, 0), (1, 0), (0, -1), (0, 1)):
        give(dx, dy)
    pump(2, 0)
    pump(2, 1)
    for h in range(2):
        for sign in ("+", "-"):
            move(h, 0, 0, "f" + sign).wait_recv()
    move_meta(0, 0, "f+").wait_recv()
    go(move_meta(1, 2, "+"))
    go(move_meta(1, 2, "-"))
    for h in range(2):
        go(move(h, 1, 2, "+"))
        go(move(h, 1, 2, "-"))
    cross(-1)
    pump(3, 0)
    cross(1)
    cross_end(0)
    for dx, dy in ((-1, -1), (-1, 1), (1, -1), (1, 1), (2, 0), (0, 2)):
        give(dx, dy)
    pump(3, 1)
    pump(4, 0)
    cross(2)
    cross_end(-1)
    cross_end(1)
    for dx, dy in ((2, -1), (2, 1), (-1, 2), (1, 2)):
        give(dx, dy)
    pump(4, 1)
    acc_q[...] = jnp.full(acc_q.shape, -1.0, jnp.float32)
    acc_k[...] = jnp.full(acc_k.shape, -1.0, jnp.float32)

    def k_columns(first, n):
        for s in range(first, first + n):
            rows = pl.ds(s * R, R)
            kcl[rows, :] = column(km[s, 0:1, :])
            kgr[rows, :] = column(km[s, 1:2, :])

    def scores(sims, j, s_cl, s_gr, l_cl, l_gr):
        s = sims[:, j * R:(j + 1) * R]
        score = jnp.where(s_cl == l_cl, s, 0.5 * s)
        return jnp.where(s_gr == l_gr, score, -1.0)

    def block(s):
        if s == 0:
            return me, z
        d = (s + 1) // 2
        return (me if s % 2 else twin), (z - d * way) & 15

    before = sub > lax.broadcasted_iota(jnp.int32, (R, R), 1)

    def groups(q, first, n, near_side):
        out = []
        for s in range(first, first + n):
            nk, zk = block(s)
            if not near_side:
                ok = (q > nk) | ((q == nk) & (z > zk))
            elif s == 0:
                ok = (q < nk) | ((q == nk) & before)
            else:
                ok = (q < nk) | ((q == nk) & (zk > z))
            out.append(jnp.where(ok, kgr[s * R:(s + 1) * R, :], -1.0))
        return jnp.concatenate(out, axis=0) if n > 1 else out[0]

    def near(t, edge):
        stream = kb[0:NEAR_SLOTS].reshape(NEAR_SLOTS * R, D)
        lanes = qb[pl.ds(t * 8, 8)].reshape(2 * TILE, D)
        sims = lax.dot_general(stream, lanes, NT, preferred_element_type=jnp.float32)
        rows = pl.ds(0, NEAR_SLOTS * R)
        best = acc_k[...]
        for j in range(8):
            q = t * 8 + j
            gr = groups(q, 0, NEAR_SLOTS, True) if edge else kgr[rows, :]
            best = jnp.maximum(best, scores(sims, j, kcl[rows, :], gr, qm[q, 0:1, :], qm[q, 1:2, :]))
        acc_k[...] = best

    def near_loop(lo, hi):
        def body(t, carry):
            near(t, False)
            return carry
        lax.fori_loop(lo, hi, body, 0)

    def far(t, first, n, edge):
        rows = pl.ds(first * R, n * R)
        stream = kb[first:first + n].reshape(n * R, D)
        lanes = qb[pl.ds(t * 8, 8)].reshape(2 * TILE, D)
        sims = lax.dot_general(stream, lanes, NT, preferred_element_type=jnp.float32)
        for j in range(8):
            q = t * 8 + j
            gr = groups(q, first, n, False) if edge else kgr[rows, :]
            best = scores(sims, j, kcl[rows, :], gr, qm[q, 0:1, :], qm[q, 1:2, :])
            where = pl.ds(pl.multiple_of(q * R, R), R)
            acc_q[:, where] = jnp.maximum(acc_q[:, where], jnp.max(best.reshape(n * R // 8, 8, R), axis=0))

    def far_loop(first, n):
        def body(t, carry):
            far(t, first, n, False)
            return carry
        lax.fori_loop(y + 1, NY, body, 0)
        far(y, first, n, True)

    def back(s):
        d, o = (s + 1) // 2, (s + 1) % 2
        at = 2 * d - 1 + c
        return rc(k_out.at[s], k_in.at[at], ns.at[s], nr.at[at], dev(dz=-d * way, flip=o == 1))

    def reply(k):
        dx, dy, flip = k % NX, (k // NX) % NY, k >= NX * NY
        return rc(q_out.at[slot(dx, dy, flip)], q_in.at[k], fs.at[k], fr.at[k], dev(dx, dy, 0, flip))

    def hops(k):
        dx, dy = k % NX, (k // NX) % NY
        return min(dx, NX - dx) + min(dy, NY - dy)

    def plane_result(k):
        dx, dy, flip = k % NX, (k // NX) % NY, k >= NX * NY
        s = slot(dx, dy, flip)
        return s, jnp.max(acc_q[:, pl.ds(pl.multiple_of(s * R, R), R)], axis=0, keepdims=True)

    k_columns(0, NEAR_SLOTS)
    for dx in range(1, NX):
        for copy in share(dx, 0):
            copy.wait_recv()
    near(y, True)
    cross_end(2)
    give(2, 2)
    pump(5, 0)
    pump(5, 1)
    k_columns(9, 2)
    for dy in range(1, NY):
        for dx in range(NX):
            for copy in share(dx, dy):
                copy.wait_recv()
    cut_a = (y + 2) // 3
    cut_b = cut_a + (y - cut_a + 1) // 2
    near_loop(0, cut_a)
    far_loop(9, 2)
    pump(6, 0)
    pump(6, 1)
    k_columns(11, 2)
    near_loop(cut_a, cut_b)
    far_loop(11, 2)
    pump(7, 0)
    pump(7, 1)
    near_loop(cut_b, y)
    for s in range(NEAR_SLOTS):
        k_out[s] = jnp.max(acc_k[s * R:(s + 1) * R, :].T, axis=0, keepdims=True)
    for s in range(1, NEAR_SLOTS):
        go(back(s))
    k_columns(13, 2)
    far_loop(13, 2)
    pump(8, 0)
    k_columns(15, 1)
    far_loop(15, 1)
    for k in sorted(range(1, PLANE), key=hops, reverse=True):
        s, result = plane_result(k)
        q_out[s] = result
        go(reply(k))
    best = jnp.maximum(k_out[0], plane_result(0)[1])
    for s in range(1, NEAR_SLOTS):
        rc(k_out.at[0], k_in.at[s], ns.at[0], nr.at[s], dev(dz=1)).wait_recv()
    for s in range(1, NEAR_SLOTS):
        best = jnp.maximum(best, k_in[s])
    for k in range(1, PLANE):
        reply(k).wait_recv()
    for k in range(1, PLANE):
        best = jnp.maximum(best, q_in[k])
    out_ref[...] = best
    for copy in pending:
        copy.wait_send()


def solution(mesh):
    def step(embeddings, cluster_id, cluster_group):
        dma = pltpu.SemaphoreType.DMA
        f32 = jnp.float32
        best = pl.pallas_call(
            kernel,
            out_shape=jax.ShapeDtypeStruct((1, R), f32),
            in_specs=[pl.BlockSpec(memory_space=pl.ANY)] * 3,
            out_specs=pl.BlockSpec(memory_space=pltpu.VMEM),
            scratch_shapes=[
                pltpu.VMEM((R, D), jnp.bfloat16),
                pltpu.VMEM((1, R), jnp.int32),
                pltpu.VMEM((1, cluster_group.shape[0]), jnp.int32),
                pltpu.VMEM((NZ, R, D), jnp.bfloat16),
                pltpu.VMEM((PLANE, R, D), jnp.bfloat16),
                pltpu.VMEM((NZ, 2, R), f32),
                pltpu.VMEM((PLANE, 2, R), f32),
                pltpu.VMEM((NZ * R, R), f32),
                pltpu.VMEM((NZ * R, R), f32),
                pltpu.VMEM((8, PLANE * R), f32),
                pltpu.VMEM((NEAR_SLOTS * R, R), f32),
                pltpu.VMEM((NEAR_SLOTS, 1, R), f32),
                pltpu.VMEM((NEAR_SLOTS, 1, R), f32),
                pltpu.VMEM((PLANE, 1, R), f32),
                pltpu.VMEM((PLANE, 1, R), f32),
                dma((3,)),
                dma((2 * sum(CHUNKS),)), dma((2 * sum(CHUNKS),)), dma((NZ,)), dma((NZ,)),
                dma((40,)), dma((40,)), dma((15,)), dma((15,)),
                dma((16,)), dma((16,)), dma((16,)), dma((16,)),
                dma((NEAR_SLOTS,)), dma((NEAR_SLOTS,)), dma((PLANE,)), dma((PLANE,)),
            ],
            compiler_params=pltpu.CompilerParams(
                collective_id=0, has_side_effects=True, vmem_limit_bytes=60 * 2**20),
        )(embeddings, cluster_id.reshape(1, R), cluster_group.reshape(1, -1))
        return best.reshape(R)

    placed = (P(("clu", "grp"), None), P(("clu", "grp")), P())
    return jax.shard_map(step, mesh=mesh, in_specs=placed, out_specs=P(("clu", "grp")), check_vma=False)
```

```python
import functools

import jax
import jax.numpy as jnp
from jax import lax
from jax.experimental import pallas as pl
from jax.experimental.pallas import tpu as pltpu
from jax.sharding import PartitionSpec as P

MESH = pl.DeviceIdType.MESH
NX, NY, NZ, NC = 4, 4, 16, 2
R, D = 128, 512
NEAR = 4
NEAR_SLOTS = 2 * NEAR + 1
PLANE = NX * NY * NC
TILE = 4 * R
NT = (((1,), (1,)), ((), ()))
CHUNKS = (0, 4, 4, 4, 4, 4, 1, 1, 1)
START = tuple(2 * sum(CHUNKS[:d]) for d in range(NZ // 2 + 1))


def kernel(
    emb_hbm, cid_hbm, table_hbm, out_ref,
    emb_ref, cid_ref, table_ref, kb, qb, km, qm, kcl, kgr, acc_q, acc_k,
    k_out, k_in, q_out, q_in,
    ins, zs, zr, zms, zmr, qs, qr, qms, qmr, ds, dr, dms, dmr, ns, nr, fs, fr,
):
    clu, grp = lax.axis_index("clu"), lax.axis_index("grp")
    x, z = clu // NZ, clu % NZ
    y, c = grp // NC, grp % NC
    row = y * NC + c
    me = row * NX + x

    def dev(dx=0, dy=0, dz=0, flip=False):
        xx, yy, zz = (x + dx) & 3, (y + dy) & 3, (z + dz) & 15
        cc = 1 - c if flip else c
        return (xx * NZ + zz, yy * NC + cc)

    def slot(dx, dy, flip=False):
        cc = 1 - c if flip else c
        return (((y + dy) & 3) * NC + cc) * NX + ((x + dx) & 3)

    fetch = [pltpu.make_async_copy(a, b, ins.at[i]) for i, (a, b) in enumerate(
        ((emb_hbm, emb_ref), (cid_hbm, cid_ref), (table_hbm, table_ref)))]
    for copy in fetch:
        copy.start()
    barrier = pltpu.get_barrier_semaphore()
    for step in (dict(dx=1), dict(dx=-1), dict(dy=1), dict(dy=-1), dict(dz=1), dict(dz=-1), dict(flip=True)):
        pl.semaphore_signal(barrier, inc=1, device_id=dev(**step), device_id_type=MESH)

    fetch[0].wait()
    values = emb_ref[...].astype(jnp.float32)
    scale = lax.rsqrt(jnp.sum(values * values, axis=1, keepdims=True) + 1e-06)
    unit = (values * scale).astype(jnp.bfloat16)
    kb[0] = unit
    qb[me] = unit
    pending = []

    def rc(src, dst, s, r, where):
        return pltpu.make_async_remote_copy(
            src_ref=src, dst_ref=dst, send_sem=s, recv_sem=r, device_id=where, device_id_type=MESH)

    def go(copy):
        copy.start()
        pending.append(copy)

    half = R // 2
    way = 1 - 2 * c
    twin = slot(0, 0, True)

    def ring(d, o, part):
        n = R // CHUNKS[d]
        rows = pl.ds(part * n, n)
        if d == 1:
            src = kb.at[0, rows] if o == 0 else qb.at[twin, rows]
        else:
            src = kb.at[2 * d - 3 + o, rows]
        i = START[d] + o * CHUNKS[d] + part
        return rc(src, kb.at[2 * d - 1 + o, rows], zs.at[i], zr.at[i], dev(dz=way))

    def ring_meta(d, o):
        if d == 1:
            src = km.at[0] if o == 0 else qm.at[twin]
        else:
            src = km.at[2 * d - 3 + o]
        i = 2 * d - 1 + o
        return rc(src, km.at[i], zms.at[i], zmr.at[i], dev(dz=way))

    def forward(d, o, lo, hi):
        for part in range(CHUNKS[d]):
            if lo < (part + 1) * (R // CHUNKS[d]) <= hi:
                go(ring(d, o, part))

    def pump(d, o):
        ring_meta(d, o).wait_recv()
        more = d < 7 or (d == 7 and o == 0)
        if more:
            go(ring_meta(d + 1, o))
        n = R // CHUNKS[d]
        for part in range(CHUNKS[d]):
            ring(d, o, part).wait_recv()
            if more:
                forward(d + 1, o, part * n, (part + 1) * n)

    def move(h, phase, other, kind):
        along_x = (h == 0) == (phase == 0)
        step = 1 if kind[-1] == "+" else -1
        lo, n = h * half, half
        off = 0
        if kind[0] == "f":
            n = half // 2
            lo += 0 if step > 0 else n
            off = -step
        if along_x:
            s = slot(off, other if phase == 1 else 0)
            target = dev(dx=step)
        else:
            s = slot(other if phase == 1 else 0, off)
            target = dev(dy=step)
        i = h * 20 + (0 if phase == 0 else 4 + 4 * (other % 4)) + ("+", "-", "f+", "f-").index(kind)
        ref = qb.at[s, pl.ds(lo, n)]
        return rc(ref, ref, qs.at[i], qr.at[i], target)

    def move_meta(phase, other, kind):
        step = -1 if kind == "-" else 1
        off = -1 if kind == "f+" else 0
        if phase == 0:
            s, target = slot(off, 0), dev(dx=step)
        else:
            s, target = slot(other, off), dev(dy=step)
        i = (0 if phase == 0 else 3 + 3 * (other % 4)) + ("+", "-", "f+").index(kind)
        return rc(qm.at[s], qm.at[s], qms.at[i], qmr.at[i], target)

    def share(dx, dy):
        s = slot(dx, dy)
        i = (dy % 4) * 4 + dx % 4
        return (rc(qb.at[s], qb.at[s], ds.at[i], dr.at[i], dev(flip=True)),
                rc(qm.at[s], qm.at[s], dms.at[i], dmr.at[i], dev(flip=True)))

    def give(dx, dy):
        for copy in share(dx, dy):
            go(copy)


    def line(off):
        sign = "+" if off < 0 else "-"
        for h in range(2):
            move(h, 0, 0, sign).wait_recv()
            go(move(h, 0, 0, "f" + sign))
        move_meta(0, 0, sign).wait_recv()
        if sign == "+":
            go(move_meta(0, 0, "f+"))
        go(move_meta(1, off, "+"))
        go(move_meta(1, off, "-"))
        for h in range(2):
            go(move(h, 1, off, "+"))
            go(move(h, 1, off, "-"))

    def cross(off):
        for sign in ("+", "-"):
            for h in range(2):
                move(h, 1, off, sign).wait_recv()
                go(move(h, 1, off, "f" + sign))
            move_meta(1, off, sign).wait_recv()
        go(move_meta(1, off, "f+"))

    def cross_end(off):
        for h in range(2):
            for sign in ("+", "-"):
                move(h, 1, off, "f" + sign).wait_recv()
        move_meta(1, off, "f+").wait_recv()

    pl.semaphore_wait(barrier, 7)
    own_share = share(0, 0)
    go(own_share[0])
    forward(1, 0, 0, R)
    for p in range(2):
        for h in range(2):
            go(move(h, p, 0, "+"))
            go(move(h, p, 0, "-"))

    fetch[1].wait()
    fetch[2].wait()
    eye = lax.broadcasted_iota(jnp.int32, (R, R), 0) == lax.broadcasted_iota(jnp.int32, (R, R), 1)
    sub = lax.broadcasted_iota(jnp.int32, (R, R), 0)
    ones = jnp.ones((R, R), jnp.bfloat16)

    def column(line):
        spread = jnp.where(eye, jnp.broadcast_to(line, (R, R)), 0.0).astype(jnp.bfloat16)
        return jnp.dot(spread, ones, preferred_element_type=jnp.float32)

    cid = cid_ref[...]
    group = jnp.zeros((1, R), jnp.float32)
    for h in range(2):
        part = column(table_ref[:, h * R:(h + 1) * R].astype(jnp.float32))
        group += jnp.sum(jnp.where(jnp.broadcast_to(cid, (R, R)) == sub + h * R, part, 0.0), axis=0, keepdims=True)
    cluster = cid.astype(jnp.float32)
    km[0, 0:1, :] = cluster
    km[0, 1:2, :] = group
    qm[me, 0:1, :] = cluster
    qm[me, 1:2, :] = group

    go(own_share[1])
    go(ring_meta(1, 0))
    for p in range(2):
        go(move_meta(p, 0, "+"))
        go(move_meta(p, 0, "-"))
    own_share[0].wait_recv()
    forward(1, 1, 0, R)
    own_share[1].wait_recv()
    go(ring_meta(1, 1))
    pump(1, 0)
    line(-1)
    line(1)
    pump(1, 1)
    cross(0)
    for dx, dy in ((-1, 0), (1, 0), (0, -1), (0, 1)):
        give(dx, dy)
    pump(2, 0)
    for h in range(2):
        for sign in ("+", "-"):
            move(h, 0, 0, "f" + sign).wait_recv()
    move_meta(0, 0, "f+").wait_recv()
    go(move_meta(1, 2, "+"))
    go(move_meta(1, 2, "-"))
    for h in range(2):
        go(move(h, 1, 2, "+"))
        go(move(h, 1, 2, "-"))
    pump(2, 1)
    cross(-1)
    pump(3, 0)
    cross(1)
    cross_end(0)
    for dx, dy in ((-1, -1), (-1, 1), (1, -1), (1, 1), (2, 0), (0, 2)):
        give(dx, dy)
    pump(3, 1)
    pump(4, 0)
    cross(2)
    cross_end(-1)
    cross_end(1)
    for dx, dy in ((2, -1), (2, 1), (-1, 2), (1, 2)):
        give(dx, dy)
    pump(4, 1)
    acc_q[...] = jnp.full(acc_q.shape, -1.0, jnp.float32)
    acc_k[...] = jnp.full(acc_k.shape, -1.0, jnp.float32)

    def k_columns(first, n):
        for s in range(first, first + n):
            rows = pl.ds(s * R, R)
            kcl[rows, :] = column(km[s, 0:1, :])
            kgr[rows, :] = column(km[s, 1:2, :])

    def scores(sims, j, s_cl, s_gr, l_cl, l_gr):
        s = sims[:, j * R:(j + 1) * R]
        score = jnp.where(s_cl == l_cl, s, 0.5 * s)
        return jnp.where(s_gr == l_gr, score, -1.0)

    def block(s):
        if s == 0:
            return me, z
        d = (s + 1) // 2
        return (me if s % 2 else twin), (z - d * way) & 15

    before = sub > lax.broadcasted_iota(jnp.int32, (R, R), 1)

    def groups(q, first, n, near_side):
        out = []
        for s in range(first, first + n):
            nk, zk = block(s)
            if not near_side:
                ok = (q > nk) | ((q == nk) & (z > zk))
            elif s == 0:
                ok = (q < nk) | ((q == nk) & before)
            else:
                ok = (q < nk) | ((q == nk) & (zk > z))
            out.append(jnp.where(ok, kgr[s * R:(s + 1) * R, :], -1.0))
        return jnp.concatenate(out, axis=0) if n > 1 else out[0]

    def near(t, edge):
        stream = kb[0:NEAR_SLOTS].reshape(NEAR_SLOTS * R, D)
        lanes = qb[pl.ds(t * 8, 8)].reshape(2 * TILE, D)
        sims = lax.dot_general(stream, lanes, NT, preferred_element_type=jnp.float32)
        rows = pl.ds(0, NEAR_SLOTS * R)
        best = acc_k[...]
        for j in range(8):
            q = t * 8 + j
            gr = groups(q, 0, NEAR_SLOTS, True) if edge else kgr[rows, :]
            best = jnp.maximum(best, scores(sims, j, kcl[rows, :], gr, qm[q, 0:1, :], qm[q, 1:2, :]))
        acc_k[...] = best

    def near_loop(lo, hi):
        def body(t, carry):
            near(t, False)
            return carry
        lax.fori_loop(lo, hi, body, 0)

    def far(t, first, n, edge):
        rows = pl.ds(first * R, n * R)
        stream = kb[first:first + n].reshape(n * R, D)
        lanes = qb[pl.ds(t * 8, 8)].reshape(2 * TILE, D)
        sims = lax.dot_general(stream, lanes, NT, preferred_element_type=jnp.float32)
        for j in range(8):
            q = t * 8 + j
            gr = groups(q, first, n, False) if edge else kgr[rows, :]
            best = scores(sims, j, kcl[rows, :], gr, qm[q, 0:1, :], qm[q, 1:2, :])
            where = pl.ds(pl.multiple_of(q * R, R), R)
            acc_q[:, where] = jnp.maximum(acc_q[:, where], jnp.max(best.reshape(n * R // 8, 8, R), axis=0))

    def far_loop(first, n):
        def body(t, carry):
            far(t, first, n, False)
            return carry
        lax.fori_loop(y + 1, NY, body, 0)
        far(y, first, n, True)

    def back(s):
        d, o = (s + 1) // 2, (s + 1) % 2
        at = 2 * d - 1 + c
        return rc(k_out.at[s], k_in.at[at], ns.at[s], nr.at[at], dev(dz=-d * way, flip=o == 1))

    def reply(k):
        dx, dy, flip = k % NX, (k // NX) % NY, k >= NX * NY
        return rc(q_out.at[slot(dx, dy, flip)], q_in.at[k], fs.at[k], fr.at[k], dev(dx, dy, 0, flip))

    def hops(k):
        dx, dy = k % NX, (k // NX) % NY
        return min(dx, NX - dx) + min(dy, NY - dy)

    def plane_result(k):
        dx, dy, flip = k % NX, (k // NX) % NY, k >= NX * NY
        s = slot(dx, dy, flip)
        return s, jnp.max(acc_q[:, pl.ds(pl.multiple_of(s * R, R), R)], axis=0, keepdims=True)

    k_columns(0, NEAR_SLOTS)
    for dx in range(1, NX):
        for copy in share(dx, 0):
            copy.wait_recv()
    near(y, True)
    cross_end(2)
    give(2, 2)
    pump(5, 0)
    pump(5, 1)
    k_columns(9, 2)
    for dy in range(1, NY):
        for dx in range(NX):
            for copy in share(dx, dy):
                copy.wait_recv()
    cut_a = (y + 2) // 3
    cut_b = cut_a + (y - cut_a + 1) // 2
    near_loop(0, cut_a)
    far_loop(9, 2)
    pump(6, 0)
    pump(6, 1)
    k_columns(11, 2)
    near_loop(cut_a, cut_b)
    far_loop(11, 2)
    pump(7, 0)
    pump(7, 1)
    near_loop(cut_b, y)
    for s in range(NEAR_SLOTS):
        k_out[s] = jnp.max(acc_k[s * R:(s + 1) * R, :].T, axis=0, keepdims=True)
    for s in range(1, NEAR_SLOTS):
        go(back(s))
    k_columns(13, 2)
    far_loop(13, 2)
    pump(8, 0)
    k_columns(15, 1)
    far_loop(15, 1)
    for k in sorted(range(1, PLANE), key=hops, reverse=True):
        s, result = plane_result(k)
        q_out[s] = result
        go(reply(k))
    best = jnp.maximum(k_out[0], plane_result(0)[1])
    for s in range(1, NEAR_SLOTS):
        rc(k_out.at[0], k_in.at[s], ns.at[0], nr.at[s], dev(dz=1)).wait_recv()
    for s in range(1, NEAR_SLOTS):
        best = jnp.maximum(best, k_in[s])
    for k in range(1, PLANE):
        reply(k).wait_recv()
    for k in range(1, PLANE):
        best = jnp.maximum(best, q_in[k])
    out_ref[...] = best
    for copy in pending:
        copy.wait_send()


def solution(mesh):
    def step(embeddings, cluster_id, cluster_group):
        dma = pltpu.SemaphoreType.DMA
        f32 = jnp.float32
        best = pl.pallas_call(
            kernel,
            out_shape=jax.ShapeDtypeStruct((1, R), f32),
            in_specs=[pl.BlockSpec(memory_space=pl.ANY)] * 3,
            out_specs=pl.BlockSpec(memory_space=pltpu.VMEM),
            scratch_shapes=[
                pltpu.VMEM((R, D), jnp.bfloat16),
                pltpu.VMEM((1, R), jnp.int32),
                pltpu.VMEM((1, cluster_group.shape[0]), jnp.int32),
                pltpu.VMEM((NZ, R, D), jnp.bfloat16),
                pltpu.VMEM((PLANE, R, D), jnp.bfloat16),
                pltpu.VMEM((NZ, 2, R), f32),
                pltpu.VMEM((PLANE, 2, R), f32),
                pltpu.VMEM((NZ * R, R), f32),
                pltpu.VMEM((NZ * R, R), f32),
                pltpu.VMEM((8, PLANE * R), f32),
                pltpu.VMEM((NEAR_SLOTS * R, R), f32),
                pltpu.VMEM((NEAR_SLOTS, 1, R), f32),
                pltpu.VMEM((NEAR_SLOTS, 1, R), f32),
                pltpu.VMEM((PLANE, 1, R), f32),
                pltpu.VMEM((PLANE, 1, R), f32),
                dma((3,)),
                dma((2 * sum(CHUNKS),)), dma((2 * sum(CHUNKS),)), dma((NZ,)), dma((NZ,)),
                dma((40,)), dma((40,)), dma((15,)), dma((15,)),
                dma((16,)), dma((16,)), dma((16,)), dma((16,)),
                dma((NEAR_SLOTS,)), dma((NEAR_SLOTS,)), dma((PLANE,)), dma((PLANE,)),
            ],
            compiler_params=pltpu.CompilerParams(
                collective_id=0, has_side_effects=True, vmem_limit_bytes=60 * 2**20),
        )(embeddings, cluster_id.reshape(1, R), cluster_group.reshape(1, -1))
        return best.reshape(R)

    placed = (P(("clu", "grp"), None), P(("clu", "grp")), P())
    return jax.shard_map(step, mesh=mesh, in_specs=placed, out_specs=P(("clu", "grp")), check_vma=False)
```
